32 devices in a mesh: groups: 2 (over x), chan: 8 (over z, y), space: 2 (over core).
Axes of the slice: x: 2, y: 2, z: 4, core: 2. Of those that a mesh axis runs over, the one named last changes fastest.
Arguments:
- cube: bfloat16 [32, 1024, 512], P(('groups', 'chan'), 'space'), parts along dimension 0, may hold values from -40 to 40
- beam_response: float32 [1024, 512], P(None, 'space'), may hold values from 0.1 to 1
- line_widths: float32 [5], replicated, may hold values from 0.6 to 3
Outputs:
- detection: bfloat16 [32, 1024, 512], P(('groups', 'chan'), 'space'), parts along dimension 0
The draws below stay inside these ranges and needn't reach their ends.
There are 2 independent parts, one for each index of `groups`. The reference program is written for one: setup_inputs(seed, part) draws one part's arguments, and reference() takes and returns one part's arrays. A program takes and returns all parts, laid end to end along the dimension named above; an argument that names none is the same for every part. Nothing has to cross between parts.
All inputs are finite; a program needn't handle non-finite values.
Results may differ from the reference program's by a relative error of at most 0.025.
Values may be sent and summed in bfloat16 or wider, within the bound.
No kernel may reach another device: no remote copies, remote signals or barrier semaphores. Data moves between devices by JAX's collectives and lax.ppermute only.
A program may use at most 128 MiB of HBM per device.

```python
import math
import jax
import jax.numpy as jnp
from jax import lax

ROWS = 1024
COLS = 512
ORDER = 8
KERNELS = 5
HALO = 2
CHANNELS = 16


def draw_cube(key, part):
    keys = jax.random.split(jax.random.fold_in(key, 17), 2)
    rowpos = jnp.arange(ROWS, dtype=jnp.int32).astype(jnp.float32) / max(ROWS - 1, 1)
    row_scale = jnp.exp(math.log(3.0) * rowpos)
    col_scale = jnp.exp(jax.random.uniform(keys[1], (COLS,), jnp.float32, 0.0, math.log(3.3)))
    base = jnp.clip(jax.random.normal(keys[0], (CHANNELS, ROWS, COLS), jnp.float32), -4.0, 4.0)
    values = base * row_scale[None, :, None] * col_scale[None, None, :]
    return values.astype(jnp.bfloat16)


def shard_levels(rng, shape, cuts, smallest, high):
    factor_of, own = 1.0, jax.random.fold_in(rng, 6)
    for dim, parts in cuts:
        steps = jnp.exp(jax.random.uniform(jax.random.fold_in(own, dim), (parts,), jnp.float32, smallest / len(cuts), high / len(cuts)))
        factor_of = factor_of * jnp.repeat(steps, shape[dim] // parts).reshape([-1 if axis == dim else 1 for axis in range(len(shape))])
    return factor_of


def setup_inputs(seed: int = 0, part: int = 0) -> dict:
    arg_keys = jax.random.split(jax.random.key(seed), 4)
    part_splits = jax.random.split(jax.random.fold_in(arg_keys[3], part), 4)
    cube = draw_cube(jax.random.fold_in(jax.random.fold_in(arg_keys[3], part), 71), part)
    beam_response = jnp.clip(0.1 + 0.9 * jax.random.uniform(arg_keys[1], (ROWS, COLS), jnp.float32) ** shard_levels(arg_keys[1], (ROWS, COLS), ((1, 2),), -0.2, 0.2), 0.1, 1.0)
    line_widths = jnp.clip(jnp.exp(jax.random.uniform(arg_keys[2], (KERNELS,), jnp.float32, math.log(0.6), math.log(3.0))), 0.6, 3.0)
    return {"cube": cube, "beam_response": beam_response, "line_widths": line_widths}


def legendre_basis(channels):
    pos = jnp.arange(channels, dtype=jnp.int32).astype(jnp.float32)
    xval = -1.0 + (2.0 * pos + 1.0) / channels
    columns = [jnp.ones_like(xval), xval]
    for degree in range(1, ORDER):
        nxt = ((2.0 * degree + 1.0) * xval * columns[degree] - degree * columns[degree - 1]) / (degree + 1.0)
        columns.append(nxt)
    done = []
    for degree in range(ORDER + 1):
        vector = columns[degree]
        for prior in done:
            vector = vector - jnp.sum(prior * vector) * prior
        vector = vector / jnp.sqrt(jnp.sum(vector * vector))
        done.append(vector)
    return jnp.stack(done, axis=1)

def dft_tables(length):
    index = jnp.arange(length, dtype=jnp.int32)
    product = index[:, None] * index[None, :] % length
    phase = product.astype(jnp.float32) * (2.0 * math.pi / length)
    return (jnp.cos(phase).astype(jnp.bfloat16), jnp.sin(phase).astype(jnp.bfloat16))

def kernel_taps(widths, reach):
    offset = jnp.arange(-reach, reach + 1, dtype=jnp.int32).astype(jnp.float32)
    shape = jnp.exp(-offset[None, :] ** 2 / (2.0 * widths[:, None] ** 2))
    return (shape / jnp.sqrt(lax.optimization_barrier(jnp.sum(shape * shape, axis=1, keepdims=True)))).astype(jnp.bfloat16)

def band_matrix(taps, count, reach):
    chans = jnp.arange(count, dtype=jnp.int32)
    padded = jnp.arange(count + 2 * reach, dtype=jnp.int32)
    offset = padded[None, :] - chans[:, None]
    picks = jnp.arange(2 * reach + 1, dtype=jnp.int32)
    onehot = (offset[:, :, None] == picks[None, None, :]).astype(jnp.float32)
    return jnp.einsum('kj,cmj->kcm', taps.astype(jnp.float32), onehot).astype(jnp.bfloat16)

def product(form, left, right):
    return jnp.einsum(form, left.astype(jnp.float32), right.astype(jnp.float32), precision=lax.Precision.HIGHEST)

def reference(cube, beam_response, line_widths):
    chans, rows, cols = cube.shape
    basis = legendre_basis(chans)
    values = cube.reshape(chans, rows * cols).astype(jnp.float32)
    coeffs = jnp.dot(basis.T, values, precision=lax.Precision.HIGHEST)
    line = (values - jnp.dot(basis, coeffs, precision=lax.Precision.HIGHEST)).astype(jnp.bfloat16)
    line = line.reshape(chans, rows, cols)
    ccos, csin = dft_tables(cols)
    rcos, rsin = dft_tables(rows)
    xreal = product('crq,qm->crm', line, ccos).astype(jnp.bfloat16)
    ximag = (-product('crq,qm->crm', line, csin)).astype(jnp.bfloat16)
    yreal = product('ur,crm->cum', rcos, xreal) + product('ur,crm->cum', rsin, ximag)
    yimag = product('ur,crm->cum', rcos, ximag) - product('ur,crm->cum', rsin, xreal)
    zreal = (yreal * beam_response[None]).astype(jnp.bfloat16)
    zimag = (yimag * beam_response[None]).astype(jnp.bfloat16)
    wreal = (product('ur,crm->cum', rcos, zreal) - product('ur,crm->cum', rsin, zimag)).astype(jnp.bfloat16)
    wimag = (product('ur,crm->cum', rcos, zimag) + product('ur,crm->cum', rsin, zreal)).astype(jnp.bfloat16)
    smooth = (product('crq,qm->crm', wreal, ccos) - product('crq,qm->crm', wimag, csin)) / (rows * cols)
    smooth = smooth.astype(jnp.bfloat16).reshape(chans, rows * cols)
    taps = kernel_taps(line_widths, HALO)
    band = band_matrix(taps, chans, HALO)
    padded = jnp.pad(smooth, ((HALO, HALO), (0, 0)))
    best = None
    for kernel in range(KERNELS):
        filtered = jnp.dot(band[kernel], padded, preferred_element_type=jnp.float32)
        noise = jnp.sqrt(lax.optimization_barrier(jnp.mean(filtered * filtered, axis=1)) + 1e-06)
        ratio = filtered / noise[:, None]
        best = ratio if best is None else jnp.maximum(best, ratio)
    return best.astype(jnp.bfloat16).reshape(chans, rows, cols)
```

```python
import functools
import math

import jax
import jax.numpy as jnp
import ml_dtypes
import numpy as np
from jax import lax
from jax.experimental import pallas as pl
from jax.experimental.pallas import tpu as pltpu
from jax.sharding import PartitionSpec as P

ORDER = 8
HALO = 2
LANES = 128
BF16 = ml_dtypes.bfloat16


def continuum_complement(channels):
    pos = np.arange(channels, dtype=np.float64)
    xval = -1.0 + (2.0 * pos + 1.0) / channels
    columns = [np.ones_like(xval), xval]
    for degree in range(1, ORDER):
        columns.append(
            ((2.0 * degree + 1.0) * xval * columns[degree] - degree * columns[degree - 1])
            / (degree + 1.0)
        )

    def orthogonal(vector, done):
        for _ in range(2):
            for prior in done:
                vector = vector - np.sum(prior * vector) * prior
        return vector

    sides = []
    for parity in (0, 1):
        done = []
        for column in columns[parity::2]:
            vector = orthogonal(column, done)
            done.append(vector / np.sqrt(np.sum(vector * vector)))
        wanted = channels // 2 - len(done)
        seeds = []
        for c in range(channels // 2):
            seed = np.zeros(channels)
            seed[c] = 1.0
            seed[channels - 1 - c] = 1.0 - 2.0 * parity
            seeds.append(seed)
        found = []
        for _ in range(wanted):
            rest = [orthogonal(seed, done) for seed in seeds]
            sizes = [float(np.sum(vector * vector)) for vector in rest]
            best = int(np.argmax(sizes))
            vector = rest[best] / math.sqrt(sizes[best])
            done.append(vector)
            found.append(vector)
        sides.append(found)
    return np.stack(sides[0] + sides[1], axis=1), len(sides[0])


def dft_table(left, right, length):
    phase = (left[:, None] * right[None, :] % length) * (2.0 * math.pi / length)
    return np.cos(phase).astype(BF16), np.sin(phase).astype(BF16)


def kernel_taps(widths, reach):
    offset = jnp.arange(-reach, reach + 1, dtype=jnp.int32).astype(jnp.float32)
    shape = jnp.exp(-offset[None, :] ** 2 / (2.0 * widths[:, None] ** 2))
    return (shape / jnp.sqrt(jnp.sum(shape * shape, axis=1, keepdims=True))).astype(jnp.bfloat16)


def iota(shape, axis):
    return lax.broadcasted_iota(jnp.int32, shape, axis)


class Plan:
    def __init__(self, chans, spaces, local_chans, local_rows, cols):
        self.chans, self.spaces = chans, spaces
        self.channels = local_chans * chans
        self.rows = local_rows * spaces
        self.cols = cols
        self.devices = chans * spaces
        self.share = self.rows // self.devices
        self.comp, self.evens = continuum_complement(self.channels)
        self.planes = self.comp.shape[1]
        self.freqs = cols // 2 // self.devices
        self.slots = LANES // self.freqs
        used = self.planes * self.freqs + self.planes
        self.tiles = -(-used // LANES)
        self.wide = self.tiles * LANES
        self.ride = (
            self.planes < self.slots
            and self.planes <= 8
            and self.freqs >= 8
            and self.share >= 32
            and self.tiles == 1
        )
        assert spaces == 2 and self.devices % self.slots == 0


def slot_of(plan, shape):
    return lax.shift_right_logical(
        iota(shape, len(shape) - 1), int(math.log2(plan.freqs))
    )


def spectra_kernel(plan, cube_ref, cos_ref, sin_ref, out_ref, fit_ref):
    share, cols, half = plan.share, plan.cols, plan.channels // 2
    lane_tiles = cols // LANES
    comp = plan.comp

    def project(step, carry):
        row = pl.multiple_of((step // lane_tiles) * 16, 16)
        col = pl.multiple_of((step % lane_tiles) * LANES, LANES)
        sums, difs = [], []
        for c in range(half):
            a = cube_ref[c, pl.ds(row, 16), pl.ds(col, LANES)].astype(jnp.float32)
            b = cube_ref[plan.channels - 1 - c, pl.ds(row, 16), pl.ds(col, LANES)].astype(
                jnp.float32
            )
            sums.append(a + b)
            difs.append(a - b)
        for j in range(plan.planes):
            parts = sums if j < plan.evens else difs
            total = None
            for c in range(half):
                term = parts[c] * float(comp[c, j])
                total = term if total is None else total + term
            fit_ref[j, pl.ds(row, 16), pl.ds(col, LANES)] = total.astype(jnp.bfloat16)
        return carry

    lax.fori_loop(0, (share // 16) * lane_tiles, project, 0)
    fits = fit_ref[...].reshape(plan.planes * share, cols)
    real = jnp.dot(fits, cos_ref[:, : cols // 2], preferred_element_type=jnp.float32)
    imag = -jnp.dot(fits, sin_ref[:, : cols // 2], preferred_element_type=jnp.float32)
    sign = (1 - 2 * (iota((cols, LANES), 0) & 1)).astype(jnp.bfloat16)
    last = jnp.dot(fits, sign, preferred_element_type=jnp.float32)
    slot = slot_of(plan, (share, LANES))
    lane = iota((share, LANES), 1)
    groups = plan.devices // plan.slots
    for part, spec in enumerate((real, imag)):
        for group in range(groups):
            turned = []
            for j in range(plan.planes):
                block = spec[j * share : (j + 1) * share, group * LANES : (group + 1) * LANES]
                shift = plan.freqs * (j % plan.slots)
                turned.append(pltpu.roll(block, shift, 1) if shift else block)
            for e in range(plan.slots):
                dest = group * plan.slots + e
                for tile in range(plan.tiles):
                    value = jnp.zeros((share, LANES), jnp.float32)
                    for j in range(tile * plan.slots, min((tile + 1) * plan.slots, plan.planes)):
                        value = jnp.where(slot == (e + j) % plan.slots, turned[j], value)
                    if dest == 0 and part == 0:
                        for j in range(plan.planes):
                            at = plan.planes * plan.freqs + j
                            if at // LANES == tile:
                                value = jnp.where(
                                    lane == at % LANES, last[j * share : (j + 1) * share], value
                                )
                    start = part * plan.wide + tile * LANES
                    out_ref[dest, :, start : start + LANES] = value.astype(jnp.bfloat16)


def lane_facts(plan, dev, shape, axis):
    lane = iota(shape, axis)
    part = (lane >= plan.wide).astype(jnp.int32)
    local = lane - part * plan.wide
    tile = lax.shift_right_logical(local, 7)
    slot = lax.shift_right_logical(local & (LANES - 1), int(math.log2(plan.freqs)))
    freq = local & (plan.freqs - 1)
    plane = tile * plan.slots + ((slot - (dev & (plan.slots - 1))) & (plan.slots - 1))
    base = plan.planes * plan.freqs
    own = (local >= base) & (local < base + plan.planes) & (dev == 0)
    plane = jnp.where(own, local - base, plane)
    freq = jnp.where(own, plan.freqs, freq)
    single = own | ((dev == 0) & (freq == 0))
    weight = jnp.where(single, (1 - part) * plan.cols, plan.cols // 2)
    return part, freq, plane, weight


def smooth_kernel(plan, dev_ref, spec_ref, ce_ref, se_ref, co_ref, so_ref, ct_ref, st_ref,
                  beam_ref, out_ref, *gram_refs):
    dev = dev_ref[0]
    half, wide, share = plan.rows // 2, plan.wide, plan.share
    low = spec_ref[:, 0].reshape(half, 2 * wide).astype(jnp.float32)
    high = spec_ref[:, 1].reshape(half, 2 * wide).astype(jnp.float32)
    waves = []
    for parity, cos, sin, icos, isin in (
        (0, ce_ref, se_ref, ce_ref, se_ref),
        (1, co_ref, so_ref, ct_ref, st_ref),
    ):
        data = ((low - high) if parity else (low + high)).astype(jnp.bfloat16)
        by_cos = jnp.dot(cos[...], data, preferred_element_type=jnp.float32)
        by_sin = jnp.dot(sin[...], data, preferred_element_type=jnp.float32)
        beam = beam_ref[parity]
        zreal = ((by_cos[:, :wide] + by_sin[:, wide:]) * beam).astype(jnp.bfloat16)
        zimag = ((by_cos[:, wide:] - by_sin[:, :wide]) * beam).astype(jnp.bfloat16)
        data = jnp.concatenate([zreal, zimag], axis=1)
        by_cos = jnp.dot(icos[...], data, preferred_element_type=jnp.float32)
        by_sin = jnp.dot(isin[...], data, preferred_element_type=jnp.float32)
        waves.append(
            (by_cos[:, :wide] - by_sin[:, wide:], by_cos[:, wide:] + by_sin[:, :wide])
        )
    (ereal, eimag), (oreal, oimag) = waves
    lows = jnp.concatenate([ereal + oreal, eimag + oimag], axis=1).astype(jnp.bfloat16)
    highs = jnp.concatenate([ereal - oreal, eimag - oimag], axis=1).astype(jnp.bfloat16)
    out_ref[:, 0] = lows.reshape(plan.chans, share, 2 * wide)
    out_ref[:, 1] = highs.reshape(plan.chans, share, 2 * wide)
    both = jnp.concatenate([lows, highs], axis=0)
    part, freq, plane, weight = lane_facts(plan, dev, (1, 2 * wide), 1)
    weighted = (both.astype(jnp.float32) * weight.astype(jnp.float32)).astype(jnp.bfloat16)
    cross = lax.dot_general(
        both, weighted, (((0,), (0,)), ((), ())), preferred_element_type=jnp.float32
    )
    cpart, cfreq, cplane, _ = lane_facts(plan, dev, (2 * wide, 1), 0)
    cross = jnp.where((part == cpart) & (freq == cfreq), cross, 0.0)
    count = -(-plan.planes // 8) * 8
    rows_of = (iota((count, 2 * wide), 0) == plane).astype(jnp.float32)
    if plan.ride:
        free = ((dev & (plan.slots - 1)) + plan.planes) & (plan.slots - 1)
        target = iota((2 * wide, LANES), 1) - free * plan.freqs
    else:
        target = iota((2 * wide, -(-plan.planes // LANES) * LANES), 1)
    cols_of = ((target == cplane) & (target < plan.planes)).astype(jnp.float32)
    high_p = lax.Precision.HIGHEST
    gram = jnp.dot(rows_of, cross, precision=high_p, preferred_element_type=jnp.float32)
    gram = jnp.dot(gram, cols_of, precision=high_p, preferred_element_type=jnp.float32)
    if plan.ride:
        first = gram.astype(jnp.bfloat16).astype(jnp.float32)
        second = (gram - first).astype(jnp.bfloat16).astype(jnp.float32)
        third = gram - first - second
        rider = jnp.concatenate([first, second, third, jnp.zeros_like(first)], axis=0)
        inside = slot_of(plan, (32, LANES)) == free
        for i in range(plan.chans):
            for s in range(plan.spaces):
                now = out_ref[i, s, 0:32, wide : 2 * wide].astype(jnp.float32)
                out_ref[i, s, 0:32, wide : 2 * wide] = jnp.where(inside, rider, now).astype(
                    jnp.bfloat16
                )
    else:
        gram_refs[0][...] = gram


def detect_kernel(plan, taps_ref, wave_ref, icos_ref, isin_ref, mix_ref, *refs):
    if plan.ride:
        out_ref, plane_ref, scale_ref = refs
    else:
        gram_ref, out_ref, plane_ref, scale_ref = refs
    share, cols, wide = plan.share, plan.cols, plan.wide
    kernels = taps_ref.shape[0]
    channels, half = plan.channels, plan.channels // 2
    groups = plan.devices // plan.slots
    slot = slot_of(plan, (share, LANES))
    lane = iota((share, LANES), 1)
    if plan.ride:
        gram = jnp.zeros((24, LANES), jnp.float32)
        free = slot_of(plan, (24, LANES))
        for e in range(plan.slots):
            at = (e + plan.planes) % plan.slots
            total = jnp.zeros((24, LANES), jnp.float32)
            for group in range(groups):
                dev = group * plan.slots + e
                total += wave_ref[dev, 0:32, wide : 2 * wide].astype(jnp.float32)[0:24]
            total = jnp.where(free == at, total, 0.0)
            shift = (LANES - at * plan.freqs) % LANES
            gram += pltpu.roll(total, shift, 1) if shift else total
        gram = gram[0:8] + gram[8:16] + gram[16:24]
        gram = jnp.concatenate([gram, jnp.zeros((LANES - 8, LANES), jnp.float32)], axis=0)
    else:
        gram = gram_ref[...]
    mix = mix_ref[...]
    power = jnp.dot(mix, gram, precision=lax.Precision.HIGHEST, preferred_element_type=jnp.float32)
    power = jnp.sum(power * mix, axis=1, keepdims=True) / (plan.rows * plan.cols)
    scale = 1.0 / jnp.sqrt(jnp.maximum(power, 0.0) + 1e-06)
    scale = jnp.broadcast_to(scale, (kernels * channels, LANES))
    for k in range(kernels):
        for c in range(channels):
            row = jnp.broadcast_to(scale[k * channels + c : k * channels + c + 1], (8, LANES))
            for j in range(HALO + 1):
                scale_ref[(c * kernels + k) * (HALO + 1) + j] = row * taps_ref[k, HALO + j]

    pieces = []
    for j in range(plan.planes):
        tile, shift = j // plan.slots, (LANES - plan.freqs * (j % plan.slots)) % LANES
        line = []
        for part in range(2):
            start = part * wide + tile * LANES
            for group in range(groups):
                value = jnp.zeros((share, LANES), jnp.float32)
                for e in range(plan.slots):
                    block = wave_ref[group * plan.slots + e, :, start : start + LANES]
                    value = jnp.where(
                        slot == (e + j) % plan.slots, block.astype(jnp.float32), value
                    )
                line.append((pltpu.roll(value, shift, 1) if shift else value).astype(jnp.bfloat16))
        at = plan.planes * plan.freqs + j
        start = at // LANES * LANES
        block = wave_ref[0, :, start : start + LANES].astype(jnp.float32)
        line.append(jnp.where(lane == at % LANES, block, 0.0).astype(jnp.bfloat16))
        pieces.append(jnp.concatenate(line, axis=1))
    data = jnp.concatenate(pieces, axis=0)
    count = cols // 2
    sign = (1 - 2 * (iota((LANES, cols), 1) & 1)).astype(jnp.bfloat16)
    smooth = (
        jnp.dot(data[:, :count], icos_ref[:count, :], preferred_element_type=jnp.float32)
        - jnp.dot(data[:, count:cols], isin_ref[:count, :], preferred_element_type=jnp.float32)
        + jnp.dot(data[:, cols:], sign, preferred_element_type=jnp.float32)
    )
    plane_ref[...] = smooth.reshape(plan.planes, share, cols)
    comp = plan.comp
    lane_tiles = cols // LANES

    def respond(step, carry):
        row = pl.multiple_of((step // lane_tiles) * 16, 16)
        col = pl.multiple_of((step % lane_tiles) * LANES, LANES)
        planes = [
            plane_ref[j, pl.ds(row, 16), pl.ds(col, LANES)].reshape(2, 8, LANES)
            for j in range(plan.planes)
        ]
        chans = [None] * channels
        for c in range(half):
            even = odd = None
            for j in range(plan.planes):
                term = planes[j] * float(comp[c, j])
                if j < plan.evens:
                    even = term if even is None else even + term
                else:
                    odd = term if odd is None else odd + term
            chans[c] = even + odd
            chans[channels - 1 - c] = even - odd
        for c in range(channels):
            sums = [chans[c]]
            for j in range(1, HALO + 1):
                low = chans[c - j] if c >= j else None
                high = chans[c + j] if c + j < channels else None
                sums.append(low + high if low is not None and high is not None else (low if high is None else high))
            best = None
            for k in range(kernels):
                value = None
                for j in range(HALO + 1):
                    term = sums[j] * scale_ref[(c * kernels + k) * (HALO + 1) + j][None]
                    value = term if value is None else value + term
                best = value if best is None else jnp.maximum(best, value)
            out_ref[c, pl.ds(row, 16), pl.ds(col, LANES)] = best.reshape(16, LANES).astype(
                jnp.bfloat16
            )
        return carry

    lax.fori_loop(0, (share // 16) * lane_tiles, respond, 0)


def call(kernel, out_shape, args, scratch=(), smem=(), name=None):
    vmem = pl.BlockSpec(memory_space=pltpu.VMEM)
    return pl.pallas_call(
        kernel,
        out_shape=out_shape,
        in_specs=[
            pl.BlockSpec(memory_space=pltpu.SMEM) if at in smem else vmem
            for at in range(len(args))
        ],
        out_specs=jax.tree.map(lambda _: vmem, out_shape),
        scratch_shapes=list(scratch),
        name=name,
    )(*args)


def own_beam(plan, beam, dev, side):
    rows, cols, freqs = plan.rows, plan.cols, plan.freqs
    other = lax.ppermute(beam, "space", [(0, 1), (1, 0)])
    low = jnp.where(side == 0, beam, other)
    high = jnp.where(side == 0, other, beam)
    direct = lax.dynamic_slice_in_dim(low, dev * freqs, freqs, axis=1)
    padded = jnp.pad(high, ((0, 0), (0, 1)))
    mirror = lax.dynamic_slice_in_dim(
        padded, cols // 2 - dev * freqs - freqs + 1, freqs, axis=1
    )[:, ::-1]
    mirror = jnp.concatenate([mirror[:1], mirror[1:][::-1]], axis=0)
    both = jnp.tile(direct + mirror, (1, plan.wide // freqs))
    own = jnp.arange(plan.wide) >= plan.planes * freqs
    both = jnp.where((dev == 0) & own[None, :], high[:, :1], both) / (rows * cols)
    return both.reshape(rows // 2, 2, plan.wide).transpose(1, 0, 2)


def local(cube, beam_response, line_widths):
    local_chans, local_rows, cols = cube.shape
    chans, spaces = lax.axis_size("chan"), lax.axis_size("space")
    plan = Plan(chans, spaces, local_chans, local_rows, cols)
    rows, share, wide, channels = plan.rows, plan.share, plan.wide, plan.channels
    side = lax.axis_index("space")
    dev = lax.axis_index("chan") * spaces + side
    half = rows // 2
    steps = np.arange(half, dtype=np.int64)
    ccos, csin = dft_table(np.arange(cols), np.arange(cols), cols)
    ecos, esin = dft_table(2 * steps, steps, rows)
    ocos, osin = dft_table(2 * steps + 1, steps, rows)
    ccos, csin, ocos, osin = (jnp.asarray(t) for t in (ccos, csin, ocos, osin))
    if half == cols:
        ecos, esin = ccos, csin
    tcos, tsin = ocos.T, osin.T

    moved = cube.reshape(local_chans, chans, share, cols).transpose(1, 0, 2, 3)
    moved = lax.all_to_all(moved, "chan", 0, 0, tiled=True)
    moved = moved.reshape(channels, share, cols)
    beam = own_beam(plan, beam_response, dev, side)
    taps = kernel_taps(line_widths, HALO).astype(jnp.float32)
    padded = np.pad(plan.comp, ((HALO, HALO), (0, 0))).astype(np.float32)
    mix = sum(taps[:, j, None, None] * padded[None, j : j + channels] for j in range(2 * HALO + 1))
    mix = mix.reshape(-1, plan.planes)
    mix = jnp.pad(mix, ((0, 0), (0, -plan.planes % LANES)))
    spectra = call(
        functools.partial(spectra_kernel, plan),
        jax.ShapeDtypeStruct((plan.devices, share, 2 * wide), jnp.bfloat16),
        (moved, ccos, csin),
        [pltpu.VMEM((plan.planes, share, cols), jnp.bfloat16)],
        name="spectra",
    )
    spectra = lax.all_to_all(spectra, ("chan", "space"), 0, 0, tiled=True)
    wave_shape = jax.ShapeDtypeStruct((chans, spaces, share, 2 * wide), jnp.bfloat16)
    gram_shape = jax.ShapeDtypeStruct(
        (-(-plan.planes // 8) * 8, -(-plan.planes // LANES) * LANES), jnp.float32
    )
    waves = call(
        functools.partial(smooth_kernel, plan),
        (wave_shape,) if plan.ride else (wave_shape, gram_shape),
        (
            dev.reshape(1).astype(jnp.int32),
            spectra.reshape(chans, spaces, share, 2 * wide),
            ecos, esin, ocos, osin, tcos, tsin, beam,
        ),
        smem=(0,),
        name="smooth",
    )
    wave = waves[0].reshape(plan.devices, share, 2 * wide)
    wave = lax.all_to_all(wave, ("chan", "space"), 0, 0, tiled=True)
    extra = ()
    if not plan.ride:
        gram = lax.psum(waves[1], ("chan", "space"))
        extra = (jnp.pad(gram, ((0, gram.shape[1] - gram.shape[0]), (0, 0))),)
    kernels = taps.shape[0]
    best = call(
        functools.partial(detect_kernel, plan),
        jax.ShapeDtypeStruct((channels, share, cols), jnp.bfloat16),
        (taps, wave, ccos, csin, mix) + extra,
        [
            pltpu.VMEM((plan.planes, share, cols), jnp.float32),
            pltpu.VMEM((channels * kernels * (HALO + 1), 8, LANES), jnp.float32),
        ],
        smem=(0,),
        name="detect",
    )
    best = best.reshape(chans, local_chans, share, cols)
    best = lax.all_to_all(best, "chan", 0, 0, tiled=True)
    return best.transpose(1, 0, 2, 3).reshape(local_chans, local_rows, cols)


def solution(mesh):
    in_specs = (P(("groups", "chan"), "space", None), P(None, "space"), P())
    out_specs = P(("groups", "chan"), "space", None)
    return jax.shard_map(local, mesh=mesh, in_specs=in_specs, out_specs=out_specs, check_vma=False)
```

```python
import functools
import math

import jax
import jax.numpy as jnp
import ml_dtypes
import numpy as np
from jax import lax
from jax.experimental import pallas as pl
from jax.experimental.pallas import tpu as pltpu
from jax.sharding import PartitionSpec as P

ORDER = 8
HALO = 2
LANES = 128
BF16 = ml_dtypes.bfloat16


def continuum_complement(channels):
    pos = np.arange(channels, dtype=np.float64)
    xval = -1.0 + (2.0 * pos + 1.0) / channels
    columns = [np.ones_like(xval), xval]
    for degree in range(1, ORDER):
        columns.append(
            ((2.0 * degree + 1.0) * xval * columns[degree] - degree * columns[degree - 1])
            / (degree + 1.0)
        )

    def orthogonal(vector, done):
        for _ in range(2):
            for prior in done:
                vector = vector - np.sum(prior * vector) * prior
        return vector

    sides = []
    for parity in (0, 1):
        done = []
        for column in columns[parity::2]:
            vector = orthogonal(column, done)
            done.append(vector / np.sqrt(np.sum(vector * vector)))
        wanted = channels // 2 - len(done)
        seeds = []
        for c in range(channels // 2):
            seed = np.zeros(channels)
            seed[c] = 1.0
            seed[channels - 1 - c] = 1.0 - 2.0 * parity
            seeds.append(seed)
        found = []
        for _ in range(wanted):
            rest = [orthogonal(seed, done) for seed in seeds]
            sizes = [float(np.sum(vector * vector)) for vector in rest]
            best = int(np.argmax(sizes))
            vector = rest[best] / math.sqrt(sizes[best])
            done.append(vector)
            found.append(vector)
        sides.append(found)
    return np.stack(sides[0] + sides[1], axis=1), len(sides[0])


def dft_table(left, right, length):
    phase = (left[:, None] * right[None, :] % length) * (2.0 * math.pi / length)
    return np.cos(phase).astype(BF16), np.sin(phase).astype(BF16)


def kernel_taps(widths, reach):
    offset = jnp.arange(-reach, reach + 1, dtype=jnp.int32).astype(jnp.float32)
    shape = jnp.exp(-offset[None, :] ** 2 / (2.0 * widths[:, None] ** 2))
    return (shape / jnp.sqrt(jnp.sum(shape * shape, axis=1, keepdims=True))).astype(jnp.bfloat16)


def iota(shape, axis):
    return lax.broadcasted_iota(jnp.int32, shape, axis)


class Plan:
    def __init__(self, chans, spaces, local_chans, local_rows, cols):
        self.chans, self.spaces = chans, spaces
        self.local_chans = local_chans
        self.channels = local_chans * chans
        self.rows = local_rows * spaces
        self.cols = cols
        self.devices = chans * spaces
        self.share = self.rows // self.devices
        self.comp, self.evens = continuum_complement(self.channels)
        self.planes = self.comp.shape[1]
        self.freqs = cols // 2 // self.devices
        self.slots = LANES // self.freqs
        used = self.planes * self.freqs + self.planes
        self.tiles = -(-used // LANES)
        self.wide = self.tiles * LANES
        self.ride = (
            self.planes < self.slots
            and self.planes <= 8
            and self.freqs >= 8
            and self.share >= 32
            and self.tiles == 1
        )
        assert spaces == 2 and self.devices % self.slots == 0 and chans & (chans - 1) == 0


def slot_of(plan, shape):
    return lax.shift_right_logical(
        iota(shape, len(shape) - 1), int(math.log2(plan.freqs))
    )


def spectra_kernel(plan, *refs):
    cubes, (comp_ref, cos_ref, sin_ref, out_ref, fit_ref) = refs[: plan.chans], refs[plan.chans :]
    share, cols, own = plan.share, plan.cols, plan.local_chans
    lane_tiles = cols // LANES

    def project(step, carry):
        row = pl.multiple_of((step // lane_tiles) * 16, 16)
        col = pl.multiple_of((step % lane_tiles) * LANES, LANES)
        sums, difs = [], []
        for k in range(plan.chans // 2):
            for c in range(own):
                one = cubes[k][c, pl.ds(row, 16), pl.ds(col, LANES)]
                two = cubes[k ^ (plan.chans - 1)][own - 1 - c, pl.ds(row, 16), pl.ds(col, LANES)]
                one, two = (v.astype(jnp.float32).reshape(2, 8, LANES) for v in (one, two))
                sums.append(one + two)
                difs.append(one - two)
        for j in range(plan.planes):
            total = None
            for at, value in enumerate(sums if j < plan.evens else difs):
                term = value * comp_ref[at * plan.planes + j][None]
                total = term if total is None else total + term
            fit_ref[j, pl.ds(row, 16), pl.ds(col, LANES)] = total.reshape(16, LANES).astype(
                jnp.bfloat16
            )
        return carry

    lax.fori_loop(0, (share // 16) * lane_tiles, project, 0)
    fits = fit_ref[...].reshape(plan.planes * share, cols)
    real = jnp.dot(fits, cos_ref[:, : cols // 2], preferred_element_type=jnp.float32)
    imag = -jnp.dot(fits, sin_ref[:, : cols // 2], preferred_element_type=jnp.float32)
    sign = (1 - 2 * (iota((cols, LANES), 0) & 1)).astype(jnp.bfloat16)
    last = jnp.dot(fits, sign, preferred_element_type=jnp.float32)
    slot = slot_of(plan, (share, LANES))
    lane = iota((share, LANES), 1)
    groups = plan.devices // plan.slots
    for part, spec in enumerate((real, imag)):
        for group in range(groups):
            turned = []
            for j in range(plan.planes):
                block = spec[j * share : (j + 1) * share, group * LANES : (group + 1) * LANES]
                shift = plan.freqs * (j % plan.slots)
                turned.append(pltpu.roll(block, shift, 1) if shift else block)
            for e in range(plan.slots):
                dest = group * plan.slots + e
                for tile in range(plan.tiles):
                    value = jnp.zeros((share, LANES), jnp.float32)
                    for j in range(tile * plan.slots, min((tile + 1) * plan.slots, plan.planes)):
                        value = jnp.where(slot == (e + j) % plan.slots, turned[j], value)
                    if dest == 0 and part == 0:
                        for j in range(plan.planes):
                            at = plan.planes * plan.freqs + j
                            if at // LANES == tile:
                                value = jnp.where(
                                    lane == at % LANES, last[j * share : (j + 1) * share], value
                                )
                    start = part * plan.wide + tile * LANES
                    out_ref[dest, :, start : start + LANES] = value.astype(jnp.bfloat16)


def lane_facts(plan, dev, shape, axis):
    lane = iota(shape, axis)
    part = (lane >= plan.wide).astype(jnp.int32)
    local = lane - part * plan.wide
    tile = lax.shift_right_logical(local, 7)
    slot = lax.shift_right_logical(local & (LANES - 1), int(math.log2(plan.freqs)))
    freq = local & (plan.freqs - 1)
    plane = tile * plan.slots + ((slot - (dev & (plan.slots - 1))) & (plan.slots - 1))
    base = plan.planes * plan.freqs
    own = (local >= base) & (local < base + plan.planes) & (dev == 0)
    plane = jnp.where(own, local - base, plane)
    freq = jnp.where(own, plan.freqs, freq)
    single = own | ((dev == 0) & (freq == 0))
    weight = jnp.where(single, (1 - part) * plan.cols, plan.cols // 2)
    return part, freq, plane, weight


def smooth_kernel(plan, dev_ref, spec_ref, ce_ref, se_ref, co_ref, so_ref, ct_ref, st_ref,
                  beam_ref, out_ref, *gram_refs):
    dev = dev_ref[0]
    half, wide, share = plan.rows // 2, plan.wide, plan.share
    low = spec_ref[:, 0].reshape(half, 2 * wide).astype(jnp.float32)
    high = spec_ref[:, 1].reshape(half, 2 * wide).astype(jnp.float32)
    waves = []
    for parity, cos, sin, icos, isin in (
        (0, ce_ref, se_ref, ce_ref, se_ref),
        (1, co_ref, so_ref, ct_ref, st_ref),
    ):
        data = ((low - high) if parity else (low + high)).astype(jnp.bfloat16)
        by_cos = jnp.dot(cos[...], data, preferred_element_type=jnp.float32)
        by_sin = jnp.dot(sin[...], data, preferred_element_type=jnp.float32)
        beam = beam_ref[parity]
        zreal = ((by_cos[:, :wide] + by_sin[:, wide:]) * beam).astype(jnp.bfloat16)
        zimag = ((by_cos[:, wide:] - by_sin[:, :wide]) * beam).astype(jnp.bfloat16)
        data = jnp.concatenate([zreal, zimag], axis=1)
        by_cos = jnp.dot(icos[...], data, preferred_element_type=jnp.float32)
        by_sin = jnp.dot(isin[...], data, preferred_element_type=jnp.float32)
        waves.append(
            (by_cos[:, :wide] - by_sin[:, wide:], by_cos[:, wide:] + by_sin[:, :wide])
        )
    (ereal, eimag), (oreal, oimag) = waves
    lows = jnp.concatenate([ereal + oreal, eimag + oimag], axis=1).astype(jnp.bfloat16)
    highs = jnp.concatenate([ereal - oreal, eimag - oimag], axis=1).astype(jnp.bfloat16)
    out_ref[:, 0] = lows.reshape(plan.chans, share, 2 * wide)
    out_ref[:, 1] = highs.reshape(plan.chans, share, 2 * wide)
    both = jnp.concatenate([lows, highs], axis=0)
    part, freq, plane, weight = lane_facts(plan, dev, (1, 2 * wide), 1)
    weighted = (both.astype(jnp.float32) * weight.astype(jnp.float32)).astype(jnp.bfloat16)
    cross = lax.dot_general(
        both, weighted, (((0,), (0,)), ((), ())), preferred_element_type=jnp.float32
    )
    cpart, cfreq, cplane, _ = lane_facts(plan, dev, (2 * wide, 1), 0)
    cross = jnp.where((part == cpart) & (freq == cfreq), cross, 0.0)
    count = -(-plan.planes // 8) * 8
    rows_of = (iota((count, 2 * wide), 0) == plane).astype(jnp.float32)
    if plan.ride:
        free = ((dev & (plan.slots - 1)) + plan.planes) & (plan.slots - 1)
        target = iota((2 * wide, LANES), 1) - free * plan.freqs
    else:
        target = iota((2 * wide, -(-plan.planes // LANES) * LANES), 1)
    cols_of = ((target == cplane) & (target < plan.planes)).astype(jnp.float32)
    high_p = lax.Precision.HIGHEST
    gram = jnp.dot(rows_of, cross, precision=high_p, preferred_element_type=jnp.float32)
    gram = jnp.dot(gram, cols_of, precision=high_p, preferred_element_type=jnp.float32)
    if plan.ride:
        first = gram.astype(jnp.bfloat16).astype(jnp.float32)
        second = (gram - first).astype(jnp.bfloat16).astype(jnp.float32)
        third = gram - first - second
        rider = jnp.concatenate([first, second, third, jnp.zeros_like(first)], axis=0)
        inside = slot_of(plan, (32, LANES)) == free
        for i in range(plan.chans):
            for s in range(plan.spaces):
                now = out_ref[i, s, 0:32, wide : 2 * wide].astype(jnp.float32)
                out_ref[i, s, 0:32, wide : 2 * wide] = jnp.where(inside, rider, now).astype(
                    jnp.bfloat16
                )
    else:
        gram_refs[0][...] = gram


def detect_kernel(plan, dev_ref, taps_ref, wave_ref, icos_ref, isin_ref, mix_ref, *refs):
    if not plan.ride:
        gram_ref, refs = refs[0], refs[1:]
    outs, (plane_ref, chan_ref, scale_ref) = refs[: plan.chans], refs[plan.chans :]
    place = lax.shift_right_logical(dev_ref[0], 1)
    share, cols, wide = plan.share, plan.cols, plan.wide
    kernels = taps_ref.shape[0]
    channels, half = plan.channels, plan.channels // 2
    groups = plan.devices // plan.slots
    slot = slot_of(plan, (share, LANES))
    lane = iota((share, LANES), 1)
    if plan.ride:
        gram = jnp.zeros((24, LANES), jnp.float32)
        free = slot_of(plan, (24, LANES))
        for e in range(plan.slots):
            at = (e + plan.planes) % plan.slots
            total = jnp.zeros((24, LANES), jnp.float32)
            for group in range(groups):
                dev = group * plan.slots + e
                total += wave_ref[dev, 0:32, wide : 2 * wide].astype(jnp.float32)[0:24]
            total = jnp.where(free == at, total, 0.0)
            shift = (LANES - at * plan.freqs) % LANES
            gram += pltpu.roll(total, shift, 1) if shift else total
        gram = gram[0:8] + gram[8:16] + gram[16:24]
        gram = jnp.concatenate([gram, jnp.zeros((LANES - 8, LANES), jnp.float32)], axis=0)
    else:
        gram = gram_ref[...]
    mix = mix_ref[...]
    power = jnp.dot(mix, gram, precision=lax.Precision.HIGHEST, preferred_element_type=jnp.float32)
    power = jnp.sum(power * mix, axis=1, keepdims=True) / (plan.rows * plan.cols)
    scale = 1.0 / jnp.sqrt(jnp.maximum(power, 0.0) + 1e-06)
    scale = jnp.broadcast_to(scale, (kernels * channels, LANES))
    for k in range(kernels):
        for c in range(channels):
            row = jnp.broadcast_to(scale[k * channels + c : k * channels + c + 1], (8, LANES))
            for j in range(HALO + 1):
                scale_ref[(c * kernels + k) * (HALO + 1) + j] = row * taps_ref[k, HALO + j]

    pieces = []
    for j in range(plan.planes):
        tile, shift = j // plan.slots, (LANES - plan.freqs * (j % plan.slots)) % LANES
        line = []
        for part in range(2):
            start = part * wide + tile * LANES
            for group in range(groups):
                value = jnp.zeros((share, LANES), jnp.float32)
                for e in range(plan.slots):
                    block = wave_ref[group * plan.slots + e, :, start : start + LANES]
                    value = jnp.where(
                        slot == (e + j) % plan.slots, block.astype(jnp.float32), value
                    )
                line.append((pltpu.roll(value, shift, 1) if shift else value).astype(jnp.bfloat16))
        at = plan.planes * plan.freqs + j
        start = at // LANES * LANES
        block = wave_ref[0, :, start : start + LANES].astype(jnp.float32)
        line.append(jnp.where(lane == at % LANES, block, 0.0).astype(jnp.bfloat16))
        pieces.append(jnp.concatenate(line, axis=1))
    data = jnp.concatenate(pieces, axis=0)
    count = cols // 2
    sign = (1 - 2 * (iota((LANES, cols), 1) & 1)).astype(jnp.bfloat16)
    smooth = (
        jnp.dot(data[:, :count], icos_ref[:count, :], preferred_element_type=jnp.float32)
        - jnp.dot(data[:, count:cols], isin_ref[:count, :], preferred_element_type=jnp.float32)
        + jnp.dot(data[:, cols:], sign, preferred_element_type=jnp.float32)
    )
    plane_ref[...] = smooth.reshape(plan.planes, share, cols)
    comp = plan.comp
    lane_tiles = cols // LANES

    own = plan.local_chans
    edge = jnp.zeros((HALO, share, cols), jnp.float32)
    chan_ref[0:HALO] = edge
    chan_ref[HALO + channels :] = edge

    def expand(step, carry):
        row = pl.multiple_of((step // lane_tiles) * 16, 16)
        col = pl.multiple_of((step % lane_tiles) * LANES, LANES)
        planes = [
            plane_ref[j, pl.ds(row, 16), pl.ds(col, LANES)].reshape(2, 8, LANES)
            for j in range(plan.planes)
        ]
        for c in range(half):
            even = odd = None
            for j in range(plan.planes):
                term = planes[j] * float(comp[c, j])
                if j < plan.evens:
                    even = term if even is None else even + term
                else:
                    odd = term if odd is None else odd + term
            for at, value in ((c, even + odd), (channels - 1 - c, even - odd)):
                chan_ref[HALO + at, pl.ds(row, 16), pl.ds(col, LANES)] = value.reshape(16, LANES)
        return carry

    def respond(step, carry):
        row = pl.multiple_of((step // lane_tiles) * 16, 16)
        col = pl.multiple_of((step % lane_tiles) * LANES, LANES)
        for block in range(plan.chans):
            first = (place ^ block) * own
            near = [
                chan_ref[first + at, pl.ds(row, 16), pl.ds(col, LANES)].reshape(2, 8, LANES)
                for at in range(own + 2 * HALO)
            ]
            for c in range(own):
                mid = c + HALO
                sums = [near[mid]]
                for j in range(1, HALO + 1):
                    sums.append(near[mid - j] + near[mid + j])
                best = None
                for k in range(kernels):
                    value = None
                    for j in range(HALO + 1):
                        at = ((first + c) * kernels + k) * (HALO + 1) + j
                        term = sums[j] * scale_ref[at][None]
                        value = term if value is None else value + term
                    best = value if best is None else jnp.maximum(best, value)
                outs[block][c, pl.ds(row, 16), pl.ds(col, LANES)] = best.reshape(
                    16, LANES
                ).astype(jnp.bfloat16)
        return carry

    lax.fori_loop(0, (share // 16) * lane_tiles, expand, 0)
    lax.fori_loop(0, (share // 16) * lane_tiles, respond, 0)


def call(kernel, out_shape, args, scratch=(), smem=(), name=None):
    vmem = pl.BlockSpec(memory_space=pltpu.VMEM)
    return pl.pallas_call(
        kernel,
        out_shape=out_shape,
        in_specs=[
            pl.BlockSpec(memory_space=pltpu.SMEM) if at in smem else vmem
            for at in range(len(args))
        ],
        out_specs=jax.tree.map(lambda _: vmem, out_shape),
        scratch_shapes=list(scratch),
        name=name,
    )(*args)


def own_beam(plan, beam, dev, side):
    rows, cols, freqs = plan.rows, plan.cols, plan.freqs
    other = lax.ppermute(beam, "space", [(0, 1), (1, 0)])
    low = jnp.where(side == 0, beam, other)
    high = jnp.where(side == 0, other, beam)
    direct = lax.dynamic_slice_in_dim(low, dev * freqs, freqs, axis=1)
    padded = jnp.pad(high, ((0, 0), (0, 1)))
    mirror = lax.dynamic_slice_in_dim(
        padded, cols // 2 - dev * freqs - freqs + 1, freqs, axis=1
    )[:, ::-1]
    mirror = jnp.concatenate([mirror[:1], mirror[1:][::-1]], axis=0)
    both = jnp.tile(direct + mirror, (1, plan.wide // freqs))
    own = jnp.arange(plan.wide) >= plan.planes * freqs
    both = jnp.where((dev == 0) & own[None, :], high[:, :1], both) / (rows * cols)
    return both.reshape(rows // 2, 2, plan.wide).transpose(1, 0, 2)


def exchange(blocks):
    count = len(blocks)
    moved = list(blocks)
    far = sorted(range(1, count), key=lambda k: -k)
    for k in far:
        moved[k] = lax.ppermute(blocks[k], "chan", [(a, a ^ k) for a in range(count)])
    return moved


def local(cube, beam_response, line_widths):
    local_chans, local_rows, cols = cube.shape
    chans, spaces = lax.axis_size("chan"), lax.axis_size("space")
    plan = Plan(chans, spaces, local_chans, local_rows, cols)
    rows, share, wide, channels = plan.rows, plan.share, plan.wide, plan.channels
    side = lax.axis_index("space")
    dev = lax.axis_index("chan") * spaces + side
    half = rows // 2
    steps = np.arange(half, dtype=np.int64)
    ccos, csin = dft_table(np.arange(cols), np.arange(cols), cols)
    ecos, esin = dft_table(2 * steps, steps, rows)
    ocos, osin = dft_table(2 * steps + 1, steps, rows)
    ccos, csin, ocos, osin = (jnp.asarray(t) for t in (ccos, csin, ocos, osin))
    if half == cols:
        ecos, esin = ccos, csin
    tcos, tsin = (lax.optimization_barrier(t).T for t in (ocos, osin))
    place = lax.axis_index("chan")

    blocks = [
        lax.dynamic_slice_in_dim(cube, (place ^ k) * share, share, axis=1) for k in range(chans)
    ]
    moved = exchange(blocks)
    pairs = plan.comp.reshape(chans, local_chans * plan.planes).astype(np.float32)
    comp = jnp.asarray(pairs)[place ^ np.arange(chans // 2)]
    comp = jnp.broadcast_to(comp.reshape(-1, 1, 1), (comp.size, 8, LANES))
    beam = own_beam(plan, beam_response, dev, side)
    taps = kernel_taps(line_widths, HALO).astype(jnp.float32)
    padded = np.pad(plan.comp, ((HALO, HALO), (0, 0))).astype(np.float32)
    mix = sum(taps[:, j, None, None] * padded[None, j : j + channels] for j in range(2 * HALO + 1))
    mix = mix.reshape(-1, plan.planes)
    mix = jnp.pad(mix, ((0, 0), (0, -plan.planes % LANES)))
    spectra = call(
        functools.partial(spectra_kernel, plan),
        jax.ShapeDtypeStruct((plan.devices, share, 2 * wide), jnp.bfloat16),
        (*moved, comp, ccos, csin),
        [pltpu.VMEM((plan.planes, share, cols), jnp.bfloat16)],
        name="spectra",
    )
    spectra = lax.all_to_all(spectra, ("chan", "space"), 0, 0, tiled=True)
    wave_shape = jax.ShapeDtypeStruct((chans, spaces, share, 2 * wide), jnp.bfloat16)
    gram_shape = jax.ShapeDtypeStruct(
        (-(-plan.planes // 8) * 8, -(-plan.planes // LANES) * LANES), jnp.float32
    )
    waves = call(
        functools.partial(smooth_kernel, plan),
        (wave_shape,) if plan.ride else (wave_shape, gram_shape),
        (
            dev.reshape(1).astype(jnp.int32),
            spectra.reshape(chans, spaces, share, 2 * wide),
            ecos, esin, ocos, osin, tcos, tsin, beam,
        ),
        smem=(0,),
        name="smooth",
    )
    wave = waves[0].reshape(plan.devices, share, 2 * wide)
    wave = lax.all_to_all(wave, ("chan", "space"), 0, 0, tiled=True)
    extra = ()
    if not plan.ride:
        gram = lax.psum(waves[1], ("chan", "space"))
        extra = (jnp.pad(gram, ((0, gram.shape[1] - gram.shape[0]), (0, 0))),)
    kernels = taps.shape[0]
    best = call(
        functools.partial(detect_kernel, plan),
        [jax.ShapeDtypeStruct((local_chans, share, cols), jnp.bfloat16)] * chans,
        (dev.reshape(1).astype(jnp.int32), taps, wave, ccos, csin, mix) + extra,
        [
            pltpu.VMEM((plan.planes, share, cols), jnp.float32),
            pltpu.VMEM((channels + 2 * HALO, share, cols), jnp.float32),
            pltpu.VMEM((channels * kernels * (HALO + 1), 8, LANES), jnp.float32),
        ],
        smem=(0, 1),
        name="detect",
    )
    out = jnp.zeros((local_chans, local_rows, cols), jnp.bfloat16)
    for k, block in enumerate(exchange(best)):
        out = lax.dynamic_update_slice_in_dim(out, block, (place ^ k) * share, axis=1)
    return out


def solution(mesh):
    in_specs = (P(("groups", "chan"), "space", None), P(None, "space"), P())
    out_specs = P(("groups", "chan"), "space", None)
    return jax.shard_map(local, mesh=mesh, in_specs=in_specs, out_specs=out_specs, check_vma=False)
```

```python
import functools
import math

import jax
import jax.numpy as jnp
import ml_dtypes
import numpy as np
from jax import lax
from jax.experimental import pallas as pl
from jax.experimental.pallas import tpu as pltpu
from jax.sharding import PartitionSpec as P

ORDER = 8
HALO = 2
LANES = 128
BF16 = ml_dtypes.bfloat16


def continuum_complement(channels):
    pos = np.arange(channels, dtype=np.float64)
    xval = -1.0 + (2.0 * pos + 1.0) / channels
    columns = [np.ones_like(xval), xval]
    for degree in range(1, ORDER):
        columns.append(
            ((2.0 * degree + 1.0) * xval * columns[degree] - degree * columns[degree - 1])
            / (degree + 1.0)
        )

    def orthogonal(vector, done):
        for _ in range(2):
            for prior in done:
                vector = vector - np.sum(prior * vector) * prior
        return vector

    sides = []
    for parity in (0, 1):
        done = []
        for column in columns[parity::2]:
            vector = orthogonal(column, done)
            done.append(vector / np.sqrt(np.sum(vector * vector)))
        wanted = channels // 2 - len(done)
        seeds = []
        for c in range(channels // 2):
            seed = np.zeros(channels)
            seed[c] = 1.0
            seed[channels - 1 - c] = 1.0 - 2.0 * parity
            seeds.append(seed)
        found = []
        for _ in range(wanted):
            rest = [orthogonal(seed, done) for seed in seeds]
            sizes = [float(np.sum(vector * vector)) for vector in rest]
            best = int(np.argmax(sizes))
            vector = rest[best] / math.sqrt(sizes[best])
            done.append(vector)
            found.append(vector)
        sides.append(found)
    return np.stack(sides[0] + sides[1], axis=1), len(sides[0])


def dft_table(left, right, length):
    phase = (left[:, None] * right[None, :] % length) * (2.0 * math.pi / length)
    return np.cos(phase).astype(BF16), np.sin(phase).astype(BF16)


def kernel_taps(widths, reach):
    offset = jnp.arange(-reach, reach + 1, dtype=jnp.int32).astype(jnp.float32)
    shape = jnp.exp(-offset[None, :] ** 2 / (2.0 * widths[:, None] ** 2))
    return (shape / jnp.sqrt(jnp.sum(shape * shape, axis=1, keepdims=True))).astype(jnp.bfloat16)


def iota(shape, axis):
    return lax.broadcasted_iota(jnp.int32, shape, axis)


class Plan:
    def __init__(self, chans, spaces, local_chans, local_rows, cols):
        self.chans, self.spaces = chans, spaces
        self.local_chans = local_chans
        self.channels = local_chans * chans
        self.rows = local_rows * spaces
        self.cols = cols
        self.devices = chans * spaces
        self.share = self.rows // self.devices
        self.comp, self.evens = continuum_complement(self.channels)
        self.planes = self.comp.shape[1]
        self.streams = cols // 2 // LANES
        self.freqs = LANES // self.devices
        self.slots = self.devices
        used = self.planes * self.freqs + self.planes
        self.packed = used <= LANES // 2
        self.tiles = -(-used // LANES)
        self.width = LANES if self.packed else 2 * self.tiles * LANES
        self.ride = self.packed and self.planes <= 8 <= self.freqs and self.share >= 32
        assert spaces == 2 and chans & (chans - 1) == 0
        assert self.freqs * self.devices == LANES and self.streams * LANES * 2 == cols

    def spot(self, part, plane):
        if self.packed:
            return 0, plane + part * self.slots // 2
        return part * self.tiles + plane // self.slots, plane % self.slots


def slot_of(plan, shape):
    return lax.shift_right_logical(
        iota(shape, len(shape) - 1), int(math.log2(plan.freqs))
    )


def spectra_kernel(plan, stream, *refs):
    share, cols, own = plan.share, plan.cols, plan.local_chans
    lane_tiles = cols // LANES
    if stream:
        fit_ref, cos_ref, sin_ref, out_ref = refs
    else:
        cubes, (comp_ref, cos_ref, sin_ref, out_ref, fit_ref) = (
            refs[: plan.chans], refs[plan.chans :]
        )

    def project(step, carry):
        row = pl.multiple_of((step // lane_tiles) * 16, 16)
        col = pl.multiple_of((step % lane_tiles) * LANES, LANES)
        sums, difs = [], []
        for k in range(plan.chans // 2):
            for c in range(own):
                one = cubes[k][c, pl.ds(row, 16), pl.ds(col, LANES)]
                two = cubes[k ^ (plan.chans - 1)][own - 1 - c, pl.ds(row, 16), pl.ds(col, LANES)]
                one, two = (v.astype(jnp.float32).reshape(2, 8, LANES) for v in (one, two))
                sums.append(one + two)
                difs.append(one - two)
        for j in range(plan.planes):
            total = None
            for at, value in enumerate(sums if j < plan.evens else difs):
                term = value * comp_ref[at * plan.planes + j][None]
                total = term if total is None else total + term
            fit_ref[j, pl.ds(row, 16), pl.ds(col, LANES)] = total.reshape(16, LANES).astype(
                jnp.bfloat16
            )
        return carry

    if stream == 0:
        lax.fori_loop(0, (share // 16) * lane_tiles, project, 0)
    fits = fit_ref[...].reshape(plan.planes * share, cols)
    mine = slice(stream * LANES, (stream + 1) * LANES)
    tables = jnp.concatenate([cos_ref[:, mine], sin_ref[:, mine]], axis=1)
    spec = jnp.dot(fits, tables, preferred_element_type=jnp.float32)
    spec = (spec[:, :LANES], -spec[:, LANES:])
    slot = slot_of(plan, (share, LANES))
    lane = iota((share, LANES), 1)
    turned = {}
    for part in range(2):
        for j in range(plan.planes):
            tile, offset = plan.spot(part, j)
            block = spec[part][j * share : (j + 1) * share]
            turned.setdefault(tile, []).append(
                (offset, pltpu.roll(block, plan.freqs * offset, 1) if offset else block)
            )
    if stream == 0:
        sign = (1 - 2 * (iota((cols, LANES), 0) & 1)).astype(jnp.bfloat16)
        last = jnp.dot(fits, sign, preferred_element_type=jnp.float32)
    for dest in range(plan.devices):
        for tile, blocks in turned.items():
            value = jnp.zeros((share, LANES), jnp.float32)
            for offset, block in blocks:
                value = jnp.where(slot == (dest + offset) % plan.slots, block, value)
            if dest == 0 and stream == 0:
                for j in range(plan.planes):
                    at = plan.planes * plan.freqs + j
                    if at // LANES == tile:
                        value = jnp.where(
                            lane == at % LANES, last[j * share : (j + 1) * share], value
                        )
            out_ref[dest, :, tile * LANES : (tile + 1) * LANES] = value.astype(jnp.bfloat16)


def lane_facts(plan, stream, dev, shape, axis):
    lane = iota(shape, axis)
    slot = lax.shift_right_logical(lane & (LANES - 1), int(math.log2(plan.freqs)))
    slot = (slot - dev) & (plan.slots - 1)
    freq = lane & (plan.freqs - 1)
    if plan.packed:
        part = (slot >= plan.slots // 2).astype(jnp.int32)
        plane = slot - part * (plan.slots // 2)
        local = lane - part * (LANES // 2)
    else:
        part = (lane >= plan.tiles * LANES).astype(jnp.int32)
        local = lane - part * plan.tiles * LANES
        plane = lax.shift_right_logical(local, 7) * plan.slots + slot
    if stream:
        return part, freq, plane, jnp.full(shape, plan.cols // 2, jnp.int32)
    base = plan.planes * plan.freqs
    own = (local >= base) & (local < base + plan.planes) & (dev == 0)
    plane = jnp.where(own, local - base, plane)
    freq = jnp.where(own, plan.freqs, freq)
    single = own | ((dev == 0) & (freq == 0))
    return part, freq, plane, jnp.where(single, (1 - part) * plan.cols, plan.cols // 2)


def smooth_kernel(plan, stream, dev_ref, spec_ref, fwd_ref, inv_ref, beam_ref, out_ref, *gram_refs):
    dev = dev_ref[0]
    quarter, width, share, half = plan.rows // 4, plan.width, plan.share, plan.chans // 2
    part, freq, plane, weight = lane_facts(plan, stream, dev, (1, width), 1)

    def turn(value):
        if plan.packed:
            return pltpu.roll(value, LANES // 2, 1) * (1 - 2 * part).astype(jnp.float32)
        return jnp.concatenate([value[:, width // 2 :], -value[:, : width // 2]], axis=1)

    x0, x1, x2, x3 = (
        spec_ref[i * half : (i + 1) * half, s].reshape(quarter, width).astype(jnp.float32)
        for s in range(2)
        for i in range(2)
    )
    a, b, c, d = x0 + x2, x1 + x3, x0 - x2, x1 - x3
    tc, td = turn(c), turn(d)
    folded = (
        (a + b, turn(a + b)), (c + td, tc - d), (a - b, turn(a - b)), (c - td, tc + d)
    )
    waves = []
    for rest, pair in enumerate(folded):
        data = jnp.concatenate(pair, axis=0).astype(jnp.bfloat16)
        value = jnp.dot(fwd_ref[rest], data, preferred_element_type=jnp.float32) * beam_ref[rest]
        data = jnp.concatenate([value, turn(value)], axis=0).astype(jnp.bfloat16)
        waves.append(jnp.dot(inv_ref[rest], data, preferred_element_type=jnp.float32))
    w0, w1, w2, w3 = waves
    even, odd, rest, side = w0 + w2, w1 + w3, w0 - w2, turn(w1 - w3)
    whole = [v.astype(jnp.bfloat16) for v in (even + odd, rest - side, even - odd, rest + side)]
    for q, value in enumerate(whole):
        i, s = q % 2, q // 2
        out_ref[i * half : (i + 1) * half, s] = value.reshape(half, share, width)
    both = jnp.concatenate(whole, axis=0)
    weighted = (both.astype(jnp.float32) * weight.astype(jnp.float32)).astype(jnp.bfloat16)
    cross = lax.dot_general(
        both, weighted, (((0,), (0,)), ((), ())), preferred_element_type=jnp.float32
    )
    cpart, cfreq, cplane, _ = lane_facts(plan, stream, dev, (width, 1), 0)
    cross = jnp.where((part == cpart) & (freq == cfreq), cross, 0.0)
    count = -(-plan.planes // 8) * 8
    rows_of = (iota((count, width), 0) == plane).astype(jnp.float32)
    if plan.ride:
        free = (dev + plan.slots // 2 + plan.planes) & (plan.slots - 1)
        target = iota((width, LANES), 1) - free * plan.freqs
    else:
        target = iota((width, -(-plan.planes // LANES) * LANES), 1)
    cols_of = ((target == cplane) & (target < plan.planes)).astype(jnp.float32)
    high_p = lax.Precision.HIGHEST
    gram = jnp.dot(rows_of, cross, precision=high_p, preferred_element_type=jnp.float32)
    gram = jnp.dot(gram, cols_of, precision=high_p, preferred_element_type=jnp.float32)
    if plan.ride:
        first = gram.astype(jnp.bfloat16).astype(jnp.float32)
        second = (gram - first).astype(jnp.bfloat16).astype(jnp.float32)
        third = gram - first - second
        rider = jnp.concatenate([first, second, third, jnp.zeros_like(first)], axis=0)
        inside = slot_of(plan, (32, LANES)) == free
        for i in range(plan.chans):
            for s in range(plan.spaces):
                now = out_ref[i, s, 0:32, :].astype(jnp.float32)
                out_ref[i, s, 0:32, :] = jnp.where(inside, rider, now).astype(jnp.bfloat16)
    else:
        gram_refs[0][...] = gram


def partial_planes(plan, stream, wave_ref, icos_ref, isin_ref):
    share, cols = plan.share, plan.cols
    slot = slot_of(plan, (share, LANES))
    lane = iota((share, LANES), 1)
    gram = None
    if plan.ride:
        gram = jnp.zeros((24, LANES), jnp.float32)
        free = slot_of(plan, (24, LANES))
        for dev in range(plan.devices):
            at = (dev + plan.slots // 2 + plan.planes) % plan.slots
            total = jnp.where(free == at, wave_ref[dev, 0:32, :].astype(jnp.float32)[0:24], 0.0)
            shift = (LANES - at * plan.freqs) % LANES
            gram += pltpu.roll(total, shift, 1) if shift else total
        gram = gram[0:8] + gram[8:16] + gram[16:24]
    loaded = {}
    for tile in range(plan.width // LANES):
        loaded[tile] = [
            wave_ref[dev, :, tile * LANES : (tile + 1) * LANES].astype(jnp.float32)
            for dev in range(plan.devices)
        ]
    pieces = []
    for j in range(plan.planes):
        line = []
        for part in range(2):
            tile, offset = plan.spot(part, j)
            value = jnp.zeros((share, LANES), jnp.float32)
            for dev in range(plan.devices):
                value = jnp.where(
                    slot == (dev + offset) % plan.slots, loaded[tile][dev], value
                )
            shift = (LANES - plan.freqs * offset) % LANES
            line.append((pltpu.roll(value, shift, 1) if shift else value).astype(jnp.bfloat16))
        if stream == 0:
            at = plan.planes * plan.freqs + j
            block = loaded[at // LANES][0]
            line.append(jnp.where(lane == at % LANES, block, 0.0).astype(jnp.bfloat16))
        pieces.append(jnp.concatenate(line, axis=1))
    data = jnp.concatenate(pieces, axis=0)
    mine = slice(stream * LANES, (stream + 1) * LANES)
    tables = jnp.concatenate([icos_ref[mine, :], -isin_ref[mine, :]], axis=0)
    smooth = jnp.dot(data[:, : 2 * LANES], tables, preferred_element_type=jnp.float32)
    if stream == 0:
        sign = (1 - 2 * (iota((LANES, cols), 1) & 1)).astype(jnp.bfloat16)
        smooth += jnp.dot(data[:, 2 * LANES :], sign, preferred_element_type=jnp.float32)
    return smooth.reshape(plan.planes, share, cols), gram


def gather_kernel(plan, stream, wave_ref, icos_ref, isin_ref, *refs):
    refs = list(refs)
    before = refs.pop(0) if stream else None
    gram_before = refs.pop(0) if stream and plan.ride else None
    smooth, gram = partial_planes(plan, stream, wave_ref, icos_ref, isin_ref)
    refs[0][...] = smooth if before is None else smooth + before[...]
    if plan.ride:
        refs[1][...] = gram if gram_before is None else gram + gram_before[...]


def detect_kernel(plan, dev_ref, taps_ref, wave_ref, icos_ref, isin_ref, before_ref, gram_ref,
                  mix_ref, *refs):
    outs, (plane_ref, chan_ref, scale_ref) = refs[: plan.chans], refs[plan.chans :]
    place = lax.shift_right_logical(dev_ref[0], 1)
    share, cols = plan.share, plan.cols
    kernels = taps_ref.shape[0]
    channels, half = plan.channels, plan.channels // 2
    smooth, gram = partial_planes(plan, plan.streams - 1, wave_ref, icos_ref, isin_ref)
    plane_ref[...] = smooth + before_ref[...]
    if plan.ride:
        gram = gram + gram_ref[...]
        gram = jnp.concatenate([gram, jnp.zeros((LANES - 8, LANES), jnp.float32)], axis=0)
    else:
        gram = gram_ref[...]
    mix = mix_ref[...]
    power = jnp.dot(mix, gram, precision=lax.Precision.HIGHEST, preferred_element_type=jnp.float32)
    power = jnp.sum(power * mix, axis=1, keepdims=True) / (plan.rows * plan.cols)
    scale = 1.0 / jnp.sqrt(jnp.maximum(power, 0.0) + 1e-06)
    scale = jnp.broadcast_to(scale, (kernels * channels, LANES))
    for k in range(kernels):
        for c in range(channels):
            row = jnp.broadcast_to(scale[k * channels + c : k * channels + c + 1], (8, LANES))
            for j in range(HALO + 1):
                scale_ref[(c * kernels + k) * (HALO + 1) + j] = row * taps_ref[k, HALO + j]

    comp = plan.comp
    lane_tiles = cols // LANES

    own = plan.local_chans
    edge = jnp.zeros((HALO, share, cols), jnp.float32)
    chan_ref[0:HALO] = edge
    chan_ref[HALO + channels :] = edge

    def expand(step, carry):
        row = pl.multiple_of((step // lane_tiles) * 16, 16)
        col = pl.multiple_of((step % lane_tiles) * LANES, LANES)
        planes = [
            plane_ref[j, pl.ds(row, 16), pl.ds(col, LANES)].reshape(2, 8, LANES)
            for j in range(plan.planes)
        ]
        for c in range(half):
            even = odd = None
            for j in range(plan.planes):
                term = planes[j] * float(comp[c, j])
                if j < plan.evens:
                    even = term if even is None else even + term
                else:
                    odd = term if odd is None else odd + term
            for at, value in ((c, even + odd), (channels - 1 - c, even - odd)):
                chan_ref[HALO + at, pl.ds(row, 16), pl.ds(col, LANES)] = value.reshape(16, LANES)
        return carry

    def respond(step, carry):
        row = pl.multiple_of((step // lane_tiles) * 16, 16)
        col = pl.multiple_of((step % lane_tiles) * LANES, LANES)
        for block in range(plan.chans):
            first = (place ^ block) * own
            near = [
                chan_ref[first + at, pl.ds(row, 16), pl.ds(col, LANES)].reshape(2, 8, LANES)
                for at in range(own + 2 * HALO)
            ]
            for c in range(own):
                mid = c + HALO
                sums = [near[mid]]
                for j in range(1, HALO + 1):
                    sums.append(near[mid - j] + near[mid + j])
                best = None
                for k in range(kernels):
                    value = None
                    for j in range(HALO + 1):
                        at = ((first + c) * kernels + k) * (HALO + 1) + j
                        term = sums[j] * scale_ref[at][None]
                        value = term if value is None else value + term
                    best = value if best is None else jnp.maximum(best, value)
                outs[block][c, pl.ds(row, 16), pl.ds(col, LANES)] = best.reshape(
                    16, LANES
                ).astype(jnp.bfloat16)
        return carry

    lax.fori_loop(0, (share // 16) * lane_tiles, expand, 0)
    lax.fori_loop(0, (share // 16) * lane_tiles, respond, 0)


def call(kernel, out_shape, args, scratch=(), smem=(), name=None):
    vmem = pl.BlockSpec(memory_space=pltpu.VMEM)
    return pl.pallas_call(
        kernel,
        out_shape=out_shape,
        in_specs=[
            pl.BlockSpec(memory_space=pltpu.SMEM) if at in smem else vmem
            for at in range(len(args))
        ],
        out_specs=jax.tree.map(lambda _: vmem, out_shape),
        scratch_shapes=list(scratch),
        name=name,
    )(*args)


def own_beam(plan, beam, dev, side):
    rows, cols, freqs, streams = plan.rows, plan.cols, plan.freqs, plan.streams
    count = streams * freqs
    at = np.arange(2 * count + 1)
    freq = (at % count) // freqs * LANES + at % freqs
    freq = freq + jnp.where(at < count, dev, dev ^ 1) * freqs
    column = jnp.where(side == 0, freq, cols // 2 - freq)
    column = jnp.where(at == 2 * count, 0, column)
    pick = (jnp.arange(cols // 2)[:, None] == column[None, :]).astype(jnp.float32)
    high_p = lax.Precision.HIGHEST
    found = jnp.dot(beam, pick, precision=high_p)
    found = found.reshape(rows // 4, 4, -1).transpose(1, 0, 2)
    flip = found[::-1, ::-1]
    flip = jnp.concatenate([jnp.roll(flip[3:], 1, axis=1), flip[:3]], axis=0)
    plain = (side == 0) | (at == 2 * count)
    found = jnp.where(plain, found, flip)
    other = lax.ppermute(found[:, :, count:], "space", [(0, 1), (1, 0)])
    total = jnp.concatenate([found[:, :, :count] + other[:, :, :count], other[:, :, count:]], axis=2)
    lane = np.arange(plan.width)
    base = plan.planes * freqs
    local = lane % (LANES // 2 if plan.packed else plan.tiles * LANES)
    own = (dev == 0) & (local >= base) & (local < base + plan.planes)
    beams = []
    for stream in range(streams):
        source = stream * freqs + lane % freqs
        if stream == 0:
            source = jnp.where(own, count, source)
        pick = (np.arange(count + 1)[:, None] == source[None, :]) * np.float32(1.0 / (rows * cols))
        beams.append(jnp.dot(total, pick, precision=high_p))
    return beams


def transpose_kernel(fwd_ref, inv_ref):
    count, size, _ = fwd_ref.shape
    for rest in range(count):
        cos = fwd_ref[rest, :, :size].astype(jnp.float32)
        sin = fwd_ref[rest, :, size:].astype(jnp.float32)
        inv_ref[rest, :, :size] = cos.T.astype(jnp.bfloat16)
        inv_ref[rest, :, size:] = (-sin.T).astype(jnp.bfloat16)


def exchange(blocks):
    count = len(blocks)
    moved = list(blocks)
    far = sorted(range(1, count), key=lambda k: -k)
    for k in far:
        moved[k] = lax.ppermute(blocks[k], "chan", [(a, a ^ k) for a in range(count)])
    return moved


def local(cube, beam_response, line_widths):
    local_chans, local_rows, cols = cube.shape
    chans, spaces = lax.axis_size("chan"), lax.axis_size("space")
    plan = Plan(chans, spaces, local_chans, local_rows, cols)
    rows, share, width, channels = plan.rows, plan.share, plan.width, plan.channels
    side = lax.axis_index("space")
    dev = lax.axis_index("chan") * spaces + side
    quarter = rows // 4
    steps = np.arange(quarter, dtype=np.int64)
    ccos, csin = dft_table(np.arange(cols), np.arange(cols), cols)
    fwd = np.stack(
        [np.concatenate(dft_table(4 * steps + rest, steps, rows), axis=1) for rest in range(4)]
    )
    ccos, csin, fwd = jnp.asarray(ccos), jnp.asarray(csin), jnp.asarray(fwd)
    place = lax.axis_index("chan")

    blocks = [
        lax.dynamic_slice_in_dim(cube, (place ^ k) * share, share, axis=1) for k in range(chans)
    ]
    moved = exchange(blocks)
    pairs = plan.comp.reshape(chans, local_chans * plan.planes).astype(np.float32)
    comp = jnp.asarray(pairs)[place ^ np.arange(chans // 2)]
    comp = jnp.broadcast_to(comp.reshape(-1, 1, 1), (comp.size, 8, LANES))
    moved[1], beam_response, table = lax.optimization_barrier((moved[1], beam_response, fwd))
    beams = own_beam(plan, beam_response, dev, side)
    inv = call(transpose_kernel, jax.ShapeDtypeStruct(fwd.shape, fwd.dtype), (table,), name="tables")
    taps = kernel_taps(line_widths, HALO).astype(jnp.float32)
    padded = np.pad(plan.comp, ((HALO, HALO), (0, 0))).astype(np.float32)
    mix = sum(taps[:, j, None, None] * padded[None, j : j + channels] for j in range(2 * HALO + 1))
    mix = mix.reshape(-1, plan.planes)
    mix = jnp.pad(mix, ((0, 0), (0, -plan.planes % LANES)))
    moved[0], beams, inv, mix, taps = lax.optimization_barrier((moved[0], beams, inv, mix, taps))
    where = dev.reshape(1).astype(jnp.int32)
    spec_shape = jax.ShapeDtypeStruct((plan.devices, share, width), jnp.bfloat16)
    fit_shape = jax.ShapeDtypeStruct((plan.planes, share, cols), jnp.bfloat16)
    wave_shape = jax.ShapeDtypeStruct((chans, spaces, share, width), jnp.bfloat16)
    gram_shape = jax.ShapeDtypeStruct(
        (-(-plan.planes // 8) * 8, -(-plan.planes // LANES) * LANES), jnp.float32
    )
    plane_shape = jax.ShapeDtypeStruct((plan.planes, share, cols), jnp.float32)
    spectra, waves, grams = [], [], []
    for stream in range(plan.streams):
        body = functools.partial(spectra_kernel, plan, stream)
        if stream == 0:
            one, fits = call(
                body, (spec_shape, fit_shape), (*moved, comp, ccos, csin), name="spectra"
            )
        else:
            one = call(body, spec_shape, (fits, ccos, csin), name="spectra")
        spectra.append(lax.all_to_all(one, ("chan", "space"), 0, 0, tiled=True))
    for stream in range(plan.streams):
        one = call(
            functools.partial(smooth_kernel, plan, stream),
            (wave_shape,) if plan.ride else (wave_shape, gram_shape),
            (where, spectra[stream].reshape(wave_shape.shape), fwd, inv, beams[stream]),
            smem=(0,),
            name="smooth",
        )
        grams.extend(one[1:])
        wave = one[0].reshape(plan.devices, share, width)
        waves.append(lax.all_to_all(wave, ("chan", "space"), 0, 0, tiled=True))
    so_far = ()
    for stream in range(plan.streams - 1):
        so_far = call(
            functools.partial(gather_kernel, plan, stream),
            (plane_shape, gram_shape) if plan.ride else (plane_shape,),
            (waves[stream], ccos, csin, *so_far),
            name="gather",
        )
    if not plan.ride:
        gram = lax.psum(sum(grams), ("chan", "space"))
        so_far = (*so_far, jnp.pad(gram, ((0, gram.shape[1] - gram.shape[0]), (0, 0))))
    kernels = taps.shape[0]
    best = call(
        functools.partial(detect_kernel, plan),
        [jax.ShapeDtypeStruct((local_chans, share, cols), jnp.bfloat16)] * chans,
        (where, taps, waves[-1], ccos, csin, *so_far, mix),
        [
            pltpu.VMEM((plan.planes, share, cols), jnp.float32),
            pltpu.VMEM((channels + 2 * HALO, share, cols), jnp.float32),
            pltpu.VMEM((channels * kernels * (HALO + 1), 8, LANES), jnp.float32),
        ],
        smem=(0, 1),
        name="detect",
    )
    out = jnp.zeros((local_chans, local_rows, cols), jnp.bfloat16)
    for k, block in enumerate(exchange(best)):
        out = lax.dynamic_update_slice_in_dim(out, block, (place ^ k) * share, axis=1)
    return out


def solution(mesh):
    in_specs = (P(("groups", "chan"), "space", None), P(None, "space"), P())
    out_specs = P(("groups", "chan"), "space", None)
    return jax.shard_map(local, mesh=mesh, in_specs=in_specs, out_specs=out_specs, check_vma=False)
```

```python
import functools
import math

import jax
import jax.numpy as jnp
import ml_dtypes
import numpy as np
from jax import lax
from jax.experimental import pallas as pl
from jax.experimental.pallas import tpu as pltpu
from jax.sharding import PartitionSpec as P

ORDER = 8
HALO = 2
LANES = 128
BF16 = ml_dtypes.bfloat16


def continuum_complement(channels):
    pos = np.arange(channels, dtype=np.float64)
    xval = -1.0 + (2.0 * pos + 1.0) / channels
    columns = [np.ones_like(xval), xval]
    for degree in range(1, ORDER):
        columns.append(
            ((2.0 * degree + 1.0) * xval * columns[degree] - degree * columns[degree - 1])
            / (degree + 1.0)
        )

    def orthogonal(vector, done):
        for _ in range(2):
            for prior in done:
                vector = vector - np.sum(prior * vector) * prior
        return vector

    sides = []
    for parity in (0, 1):
        done = []
        for column in columns[parity::2]:
            vector = orthogonal(column, done)
            done.append(vector / np.sqrt(np.sum(vector * vector)))
        wanted = channels // 2 - len(done)
        seeds = []
        for c in range(channels // 2):
            seed = np.zeros(channels)
            seed[c] = 1.0
            seed[channels - 1 - c] = 1.0 - 2.0 * parity
            seeds.append(seed)
        found = []
        for _ in range(wanted):
            rest = [orthogonal(seed, done) for seed in seeds]
            sizes = [float(np.sum(vector * vector)) for vector in rest]
            best = int(np.argmax(sizes))
            vector = rest[best] / math.sqrt(sizes[best])
            done.append(vector)
            found.append(vector)
        sides.append(found)
    return np.stack(sides[0] + sides[1], axis=1), len(sides[0])


def dft_table(left, right, length):
    phase = (left[:, None] * right[None, :] % length) * (2.0 * math.pi / length)
    return np.cos(phase).astype(BF16), np.sin(phase).astype(BF16)


def kernel_taps(widths, reach):
    offset = jnp.arange(-reach, reach + 1, dtype=jnp.int32).astype(jnp.float32)
    shape = jnp.exp(-offset[None, :] ** 2 / (2.0 * widths[:, None] ** 2))
    return (shape / jnp.sqrt(jnp.sum(shape * shape, axis=1, keepdims=True))).astype(jnp.bfloat16)


def iota(shape, axis):
    return lax.broadcasted_iota(jnp.int32, shape, axis)


class Plan:
    def __init__(self, chans, spaces, local_chans, local_rows, cols):
        self.chans, self.spaces = chans, spaces
        self.local_chans = local_chans
        self.channels = local_chans * chans
        self.rows = local_rows * spaces
        self.cols = cols
        self.share = local_rows // chans
        self.comp, self.evens = continuum_complement(self.channels)
        self.planes = self.comp.shape[1]
        self.freqs = cols // 2 // chans
        self.slots = LANES // self.freqs
        self.groups = chans // self.slots
        self.part = -(-(self.planes * self.freqs + self.planes) // LANES) * LANES
        self.width = 2 * self.part
        self.gram_rows = -(-self.planes // 8) * 8
        self.gram_cols = -(-self.planes // LANES) * LANES
        self.ride = (
            self.planes <= 8 <= self.freqs
            and self.planes < self.part // self.freqs
            and self.share >= 32
        )
        assert spaces == 2 and chans & (chans - 1) == 0 and self.groups * self.slots == chans


def slot_of(plan, shape):
    return lax.shift_right_logical(
        iota(shape, len(shape) - 1), int(math.log2(plan.freqs))
    )


def cut_kernel(plan, place_ref, cube_ref, *refs):
    outs, sems = refs[: plan.chans], refs[plan.chans]
    copies = []
    for k in range(plan.chans):
        row = pl.multiple_of((place_ref[0] ^ k) * plan.share, plan.share)
        copies.append(
            pltpu.make_async_copy(cube_ref.at[:, pl.ds(row, plan.share), :], outs[k], sems.at[k])
        )
    for copy in copies:
        copy.start()
    for copy in copies:
        copy.wait()


def spectra_kernel(plan, place_ref, *refs):
    cubes, refs = refs[: plan.chans], refs[plan.chans :]
    comp_ref, cos_ref, sin_ref = refs[:3]
    outs, (fit_ref, block_ref) = refs[3 : 3 + plan.chans], refs[3 + plan.chans :]
    share, cols, own = plan.share, plan.cols, plan.local_chans
    lane_tiles = cols // LANES

    def project(step, carry):
        row = pl.multiple_of((step // lane_tiles) * 16, 16)
        col = pl.multiple_of((step % lane_tiles) * LANES, LANES)
        sums, difs = [], []
        for k in range(plan.chans // 2):
            for c in range(own):
                one = cubes[k][c, pl.ds(row, 16), pl.ds(col, LANES)]
                two = cubes[k ^ (plan.chans - 1)][own - 1 - c, pl.ds(row, 16), pl.ds(col, LANES)]
                one, two = (v.astype(jnp.float32).reshape(2, 8, LANES) for v in (one, two))
                sums.append(one + two)
                difs.append(one - two)
        for j in range(plan.planes):
            total = None
            for at, value in enumerate(sums if j < plan.evens else difs):
                term = value * comp_ref[at * plan.planes + j][None]
                total = term if total is None else total + term
            fit_ref[j, pl.ds(row, 16), pl.ds(col, LANES)] = total.reshape(16, LANES).astype(
                jnp.bfloat16
            )
        return carry

    lax.fori_loop(0, (share // 16) * lane_tiles, project, 0)
    fits = fit_ref[...].reshape(plan.planes * share, cols)
    real = jnp.dot(fits, cos_ref[:, : cols // 2], preferred_element_type=jnp.float32)
    imag = -jnp.dot(fits, sin_ref[:, : cols // 2], preferred_element_type=jnp.float32)
    sign = (1 - 2 * (iota((cols, LANES), 0) & 1)).astype(jnp.bfloat16)
    last = jnp.dot(fits, sign, preferred_element_type=jnp.float32)
    slot = slot_of(plan, (share, LANES))
    lane = iota((share, LANES), 1)
    for part, spec in enumerate((real, imag)):
        for group in range(plan.groups):
            turned = []
            for j in range(plan.planes):
                block = spec[j * share : (j + 1) * share, group * LANES : (group + 1) * LANES]
                shift = plan.freqs * (j % plan.slots)
                turned.append(pltpu.roll(block, shift, 1) if shift else block)
            for e in range(plan.slots):
                dest = group * plan.slots + e
                for tile in range(plan.part // LANES):
                    value = jnp.zeros((share, LANES), jnp.float32)
                    for j in range(tile * plan.slots, min((tile + 1) * plan.slots, plan.planes)):
                        value = jnp.where(slot == (e + j) % plan.slots, turned[j], value)
                    if dest == 0 and part == 0:
                        for j in range(plan.planes):
                            at = plan.planes * plan.freqs + j
                            if at // LANES == tile:
                                value = jnp.where(
                                    lane == at % LANES, last[j * share : (j + 1) * share], value
                                )
                    start = part * plan.part + tile * LANES
                    block_ref[dest, :, start : start + LANES] = value.astype(jnp.bfloat16)
    for k in range(plan.chans):
        outs[k][...] = block_ref[place_ref[0] ^ k]


def lane_facts(plan, place, shape, axis):
    lane = iota(shape, axis)
    part = (lane >= plan.part).astype(jnp.int32)
    local = lane - part * plan.part
    slot = lax.shift_right_logical(local & (LANES - 1), int(math.log2(plan.freqs)))
    plane = lax.shift_right_logical(local, 7) * plan.slots + ((slot - place) & (plan.slots - 1))
    freq = local & (plan.freqs - 1)
    base = plan.planes * plan.freqs
    own = (local >= base) & (local < base + plan.planes) & (place == 0)
    plane = jnp.where(own, local - base, plane)
    freq = jnp.where(own, plan.freqs, freq)
    single = own | ((place == 0) & (freq == 0))
    return part, freq, plane, jnp.where(single, (1 - part) * plan.cols, plan.cols // 2)


def rider_of(gram):
    first = gram.astype(jnp.bfloat16).astype(jnp.float32)
    second = (gram - first).astype(jnp.bfloat16).astype(jnp.float32)
    third = gram - first - second
    return jnp.concatenate([first, second, third, jnp.zeros_like(first)], axis=0)


def free_tile(plan):
    return plan.part + plan.planes // plan.slots * LANES


def smooth_kernel(plan, place_ref, side_ref, fwd_ref, inv_ref, beam_ref, *refs):
    count = plan.chans
    mine, theirs, refs = refs[:count], refs[count : 2 * count], refs[2 * count :]
    out_ref, gram_ref, fold_ref = refs
    place, side = place_ref[0], side_ref[0]
    quarter, width, share, half = plan.rows // 4, plan.width, plan.share, plan.chans // 2
    odd = side.astype(jnp.float32)
    even = 1.0 - odd
    sigma = even - odd

    def turn(value):
        return jnp.concatenate([value[:, plan.part :], -value[:, : plan.part]], axis=1)

    for k in range(count):
        fold_ref[place ^ k] = theirs[k][...].astype(jnp.float32) + sigma * mine[k][...].astype(
            jnp.float32
        )
    low = fold_ref[0:half].reshape(quarter, width)
    high = fold_ref[half:].reshape(quarter, width)
    high = even * high + odd * turn(high)
    waves = []
    for at, value in enumerate((low + high, low - high)):
        data = jnp.concatenate([value, turn(value)], axis=0).astype(jnp.bfloat16)
        value = jnp.dot(fwd_ref[2 * side + at], data, preferred_element_type=jnp.float32)
        value = value * beam_ref[at]
        data = jnp.concatenate([value, turn(value)], axis=0).astype(jnp.bfloat16)
        waves.append(
            jnp.dot(inv_ref[2 * side + at], data, preferred_element_type=jnp.float32)
        )
    rest = waves[0] - waves[1]
    low = (waves[0] + waves[1]).astype(jnp.bfloat16)
    high = (even * rest - odd * turn(rest)).astype(jnp.bfloat16)
    out_ref[0:half] = low.reshape(half, share, width)
    out_ref[half:] = high.reshape(half, share, width)
    both = jnp.concatenate([low, high], axis=0)
    part, freq, plane, weight = lane_facts(plan, place, (1, width), 1)
    _, cfreq, cplane, _ = lane_facts(plan, place, (width, 1), 0)
    weighted = both * (2 * weight).astype(jnp.bfloat16)
    high_p = lax.Precision.HIGHEST
    if plan.ride:
        free = (place + plan.planes) & (plan.slots - 1)
    else:
        free = 0
    gram = None
    for at in range(2):
        lanes = slice(at * plan.part, (at + 1) * plan.part)
        cross = lax.dot_general(
            both[:, lanes], weighted[:, lanes], (((0,), (0,)), ((), ())),
            preferred_element_type=jnp.float32,
        )
        cross = jnp.where(freq[:, lanes] == cfreq[lanes], cross, 0.0)
        rows_of = (iota((plan.gram_rows, plan.part), 0) == plane[:, lanes]).astype(jnp.float32)
        target = iota((plan.part, plan.gram_cols), 1) - free * plan.freqs
        cols_of = ((target == cplane[lanes]) & (target < plan.planes)).astype(jnp.float32)
        cross = jnp.dot(rows_of, cross, precision=high_p, preferred_element_type=jnp.float32)
        cross = jnp.dot(cross, cols_of, precision=high_p, preferred_element_type=jnp.float32)
        gram = cross if gram is None else gram + cross
    gram_ref[...] = gram
    if plan.ride:
        tile = slice(free_tile(plan), free_tile(plan) + LANES)
        inside = slot_of(plan, (32, LANES)) == free
        now = out_ref[0, 0:32, tile].astype(jnp.float32)
        out_ref[0, 0:32, tile] = jnp.where(inside, rider_of(gram), now).astype(jnp.bfloat16)


def merge_kernel(plan, place_ref, side_ref, mine_ref, theirs_ref, gram_ref, *outs):
    place = place_ref[0]
    sigma = 1.0 - 2.0 * side_ref[0].astype(jnp.float32)
    for k in range(plan.chans):
        at = place ^ k
        value = theirs_ref[at].astype(jnp.float32) + sigma * mine_ref[at].astype(jnp.float32)
        outs[k][...] = value.astype(jnp.bfloat16)
    if plan.ride:
        tile = slice(free_tile(plan), free_tile(plan) + LANES)
        inside = slot_of(plan, (32, LANES)) == ((place + plan.planes) & (plan.slots - 1))
        other = theirs_ref[0, 0:32, tile].astype(jnp.float32)
        rider = rider_of(gram_ref[...] + other[0:8] + other[8:16] + other[16:24])
        for k in range(plan.chans):
            now = outs[k][0:32, tile].astype(jnp.float32)
            outs[k][0:32, tile] = jnp.where(inside, rider, now).astype(jnp.bfloat16)


def smooth_planes(plan, place, blocks, wave_ref, icos_ref, isin_ref):
    share, cols = plan.share, plan.cols
    for k in range(plan.chans):
        wave_ref[place ^ k] = blocks[k][...]
    slot = slot_of(plan, (share, LANES))
    lane = iota((share, LANES), 1)
    gram = None
    if plan.ride:
        gram = jnp.zeros((24, LANES), jnp.float32)
        free = slot_of(plan, (24, LANES))
        tile = slice(free_tile(plan), free_tile(plan) + LANES)
        for e in range(plan.slots):
            at = (e + plan.planes) % plan.slots
            total = jnp.zeros((24, LANES), jnp.float32)
            for group in range(plan.groups):
                block = wave_ref[group * plan.slots + e, 0:32, tile]
                total += block.astype(jnp.float32)[0:24]
            total = jnp.where(free == at, total, 0.0)
            shift = (LANES - at * plan.freqs) % LANES
            gram += pltpu.roll(total, shift, 1) if shift else total
        gram = gram[0:8] + gram[8:16] + gram[16:24]
        gram = jnp.concatenate([gram, jnp.zeros((LANES - 8, LANES), jnp.float32)], axis=0)
    pieces = []
    for j in range(plan.planes):
        tile, shift = j // plan.slots, (LANES - plan.freqs * (j % plan.slots)) % LANES
        line = []
        for part in range(2):
            start = part * plan.part + tile * LANES
            for group in range(plan.groups):
                value = jnp.zeros((share, LANES), jnp.float32)
                for e in range(plan.slots):
                    block = wave_ref[group * plan.slots + e, :, start : start + LANES]
                    value = jnp.where(
                        slot == (e + j) % plan.slots, block.astype(jnp.float32), value
                    )
                line.append((pltpu.roll(value, shift, 1) if shift else value).astype(jnp.bfloat16))
        at = plan.planes * plan.freqs + j
        start = at // LANES * LANES
        block = wave_ref[0, :, start : start + LANES].astype(jnp.float32)
        line.append(jnp.where(lane == at % LANES, block, 0.0).astype(jnp.bfloat16))
        pieces.append(jnp.concatenate(line, axis=1))
    data = jnp.concatenate(pieces, axis=0)
    count = cols // 2
    sign = (1 - 2 * (iota((LANES, cols), 1) & 1)).astype(jnp.bfloat16)
    smooth = (
        jnp.dot(data[:, :count], icos_ref[:count, :], preferred_element_type=jnp.float32)
        - jnp.dot(data[:, count:cols], isin_ref[:count, :], preferred_element_type=jnp.float32)
        + jnp.dot(data[:, cols:], sign, preferred_element_type=jnp.float32)
    )
    return smooth.reshape(plan.planes, share, cols), gram


def detect_kernel(plan, place_ref, taps_ref, icos_ref, isin_ref, mix_ref, *refs):
    blocks, refs = refs[: plan.chans], refs[plan.chans :]
    if not plan.ride:
        gram_ref, refs = refs[0], refs[1:]
    outs, (plane_ref, chan_ref, scale_ref, wave_ref) = refs[: plan.chans], refs[plan.chans :]
    place = place_ref[0]
    share, cols = plan.share, plan.cols
    kernels = taps_ref.shape[0]
    channels, half = plan.channels, plan.channels // 2
    smooth, gram = smooth_planes(plan, place, blocks, wave_ref, icos_ref, isin_ref)
    plane_ref[...] = smooth
    if not plan.ride:
        gram = gram_ref[...]
    mix = mix_ref[...]
    power = jnp.dot(mix, gram, precision=lax.Precision.HIGHEST, preferred_element_type=jnp.float32)
    power = jnp.sum(power * mix, axis=1, keepdims=True) / (plan.rows * plan.cols)
    scale = 1.0 / jnp.sqrt(jnp.maximum(power, 0.0) + 1e-06)
    scale = jnp.broadcast_to(scale, (kernels * channels, LANES))
    for k in range(kernels):
        for c in range(channels):
            row = jnp.broadcast_to(scale[k * channels + c : k * channels + c + 1], (8, LANES))
            for j in range(HALO + 1):
                scale_ref[(c * kernels + k) * (HALO + 1) + j] = row * taps_ref[k, HALO + j]

    comp = plan.comp
    lane_tiles = cols // LANES

    own = plan.local_chans
    edge = jnp.zeros((HALO, share, cols), jnp.float32)
    chan_ref[0:HALO] = edge
    chan_ref[HALO + channels :] = edge

    def expand(step, carry):
        row = pl.multiple_of((step // lane_tiles) * 16, 16)
        col = pl.multiple_of((step % lane_tiles) * LANES, LANES)
        planes = [
            plane_ref[j, pl.ds(row, 16), pl.ds(col, LANES)].reshape(2, 8, LANES)
            for j in range(plan.planes)
        ]
        for c in range(half):
            even = odd = None
            for j in range(plan.planes):
                term = planes[j] * float(comp[c, j])
                if j < plan.evens:
                    even = term if even is None else even + term
                else:
                    odd = term if odd is None else odd + term
            for at, value in ((c, even + odd), (channels - 1 - c, even - odd)):
                chan_ref[HALO + at, pl.ds(row, 16), pl.ds(col, LANES)] = value.reshape(16, LANES)
        return carry

    def respond(step, carry):
        row = pl.multiple_of((step // lane_tiles) * 16, 16)
        col = pl.multiple_of((step % lane_tiles) * LANES, LANES)
        for block in range(plan.chans):
            first = (place ^ block) * own
            near = [
                chan_ref[first + at, pl.ds(row, 16), pl.ds(col, LANES)].reshape(2, 8, LANES)
                for at in range(own + 2 * HALO)
            ]
            for c in range(own):
                mid = c + HALO
                sums = [near[mid]]
                for j in range(1, HALO + 1):
                    sums.append(near[mid - j] + near[mid + j])
                best = None
                for k in range(kernels):
                    value = None
                    for j in range(HALO + 1):
                        at = ((first + c) * kernels + k) * (HALO + 1) + j
                        term = sums[j] * scale_ref[at][None]
                        value = term if value is None else value + term
                    best = value if best is None else jnp.maximum(best, value)
                outs[block][c, pl.ds(row, 16), pl.ds(col, LANES)] = best.reshape(
                    16, LANES
                ).astype(jnp.bfloat16)
        return carry

    lax.fori_loop(0, (share // 16) * lane_tiles, expand, 0)
    lax.fori_loop(0, (share // 16) * lane_tiles, respond, 0)


def call(kernel, out_shape, args, scratch=(), smem=(), hbm=(), name=None):
    vmem = pl.BlockSpec(memory_space=pltpu.VMEM)
    return pl.pallas_call(
        kernel,
        out_shape=out_shape,
        in_specs=[
            pl.BlockSpec(memory_space=pltpu.SMEM if at in smem else pl.ANY if at in hbm else pltpu.VMEM)
            for at in range(len(args))
        ],
        out_specs=jax.tree.map(lambda _: vmem, out_shape),
        scratch_shapes=list(scratch),
        name=name,
    )(*args)


def own_beam(plan, beam, place, side):
    rows, cols, freqs = plan.rows, plan.cols, plan.freqs
    at = np.arange(freqs + 1)
    freq = place * freqs + at
    column = jnp.where(side == 0, freq, cols // 2 - freq)
    column = jnp.where(at == freqs, 0, column)
    pick = (jnp.arange(cols // 2)[:, None] == column[None, :]).astype(jnp.float32)
    high_p = lax.Precision.HIGHEST
    found = jnp.dot(beam, pick, precision=high_p)
    found = found.reshape(rows // 4, 4, -1).transpose(1, 0, 2)
    flip = found[::-1, ::-1]
    flip = jnp.concatenate([jnp.roll(flip[3:], 1, axis=1), flip[:3]], axis=0)
    plain = (side == 0) | (at == freqs)
    found = jnp.where(plain, found, flip)
    found = found.reshape(2, 2, rows // 4, freqs + 1)
    mine = jnp.where(side == 0, found[:, 0], found[:, 1])
    yours = jnp.where(side == 0, found[:, 1], found[:, 0])
    other = lax.ppermute(yours, "space", [(0, 1), (1, 0)])
    last = jnp.where(side == 0, other, mine)[:, :, freqs:]
    total = jnp.concatenate([(mine + other)[:, :, :freqs], last], axis=2)
    lane = np.arange(plan.width)
    base = plan.planes * freqs
    local = lane % plan.part
    own = (place == 0) & (local >= base) & (local < base + plan.planes)
    source = jnp.where(own, freqs, lane % freqs)
    pick = (np.arange(freqs + 1)[:, None] == source[None, :]) * np.float32(1.0 / (rows * cols))
    return jnp.dot(total, pick, precision=high_p)


def transpose_kernel(fwd_ref, inv_ref):
    count, size, _ = fwd_ref.shape
    for rest in range(count):
        cos = fwd_ref[rest, :, :size].astype(jnp.float32)
        sin = fwd_ref[rest, :, size:].astype(jnp.float32)
        inv_ref[rest, :, :size] = cos.T.astype(jnp.bfloat16)
        inv_ref[rest, :, size:] = (-sin.T).astype(jnp.bfloat16)


def exchange(blocks):
    count = len(blocks)
    moved = list(blocks)
    for k in (*range(count // 2, count), *range(count // 4, count // 2), *range(1, count // 4)):
        moved[k] = lax.ppermute(blocks[k], "chan", [(a, a ^ k) for a in range(count)])
    return moved


def swap(block):
    return lax.ppermute(block, "space", [(0, 1), (1, 0)])


def local(cube, beam_response, line_widths):
    local_chans, local_rows, cols = cube.shape
    chans, spaces = lax.axis_size("chan"), lax.axis_size("space")
    plan = Plan(chans, spaces, local_chans, local_rows, cols)
    rows, share, width, channels = plan.rows, plan.share, plan.width, plan.channels
    side, place = lax.axis_index("space"), lax.axis_index("chan")
    sides, places = (v.reshape(1).astype(jnp.int32) for v in (side, place))
    steps = np.arange(rows // 4, dtype=np.int64)
    ccos, csin = dft_table(np.arange(cols), np.arange(cols), cols)
    fwd = [np.concatenate(dft_table(4 * steps + r, steps, rows), axis=1) for r in (0, 2, 1, 3)]
    ccos, csin, fwd = jnp.asarray(ccos), jnp.asarray(csin), jnp.asarray(np.stack(fwd))

    cube_shape = jax.ShapeDtypeStruct((local_chans, share, cols), jnp.bfloat16)
    block_shape = jax.ShapeDtypeStruct((share, width), jnp.bfloat16)
    wave_shape = jax.ShapeDtypeStruct((chans, share, width), jnp.bfloat16)
    gram_shape = jax.ShapeDtypeStruct((plan.gram_rows, plan.gram_cols), jnp.float32)
    blocks = call(
        functools.partial(cut_kernel, plan), [cube_shape] * chans, (places, cube),
        [pltpu.SemaphoreType.DMA((chans,))], smem=(0,), hbm=(1,), name="cut",
    )
    moved = exchange(blocks)
    first = chans // 2
    moved[first], beam_response, table, widths = lax.optimization_barrier(
        (moved[first], beam_response, fwd, line_widths)
    )
    pairs = plan.comp.reshape(chans, local_chans * plan.planes).astype(np.float32)
    comp = jnp.asarray(pairs)[place ^ np.arange(chans // 2)]
    comp = jnp.broadcast_to(comp.reshape(-1, 1, 1), (comp.size, 8, LANES))
    beam = own_beam(plan, beam_response, place, side)
    inv = call(transpose_kernel, jax.ShapeDtypeStruct(fwd.shape, fwd.dtype), (table,), name="tables")
    taps = kernel_taps(widths, HALO).astype(jnp.float32)
    padded = np.pad(plan.comp, ((HALO, HALO), (0, 0))).astype(np.float32)
    mix = sum(taps[:, j, None, None] * padded[None, j : j + channels] for j in range(2 * HALO + 1))
    mix = mix.reshape(-1, plan.planes)
    mix = jnp.pad(mix, ((0, 0), (0, -plan.planes % LANES)))
    moved[0], beam, inv, mix, taps, comp = lax.optimization_barrier(
        (moved[0], beam, inv, mix, taps, comp)
    )
    spectra = call(
        functools.partial(spectra_kernel, plan), [block_shape] * chans,
        (places, *moved, comp, ccos, csin),
        [
            pltpu.VMEM((plan.planes, share, cols), jnp.bfloat16),
            pltpu.VMEM((chans, share, width), jnp.bfloat16),
        ],
        smem=(0,), name="spectra",
    )
    spectra = exchange(spectra)
    theirs = [swap(block) for block in spectra]
    wave, gram = call(
        functools.partial(smooth_kernel, plan), (wave_shape, gram_shape),
        (places, sides, fwd, inv, beam, *spectra, *theirs),
        [pltpu.VMEM((chans, share, width), jnp.float32)], smem=(0, 1), name="smooth",
    )
    waves = call(
        functools.partial(merge_kernel, plan), [block_shape] * chans,
        (places, sides, wave, swap(wave), gram), smem=(0, 1), name="merge",
    )
    waves = exchange(waves)
    extra = ()
    if not plan.ride:
        gram = lax.psum(gram, ("chan", "space"))
        extra = (jnp.pad(gram, ((0, gram.shape[1] - gram.shape[0]), (0, 0))),)
    kernels = taps.shape[0]
    best = call(
        functools.partial(detect_kernel, plan), [cube_shape] * chans,
        (places, taps, ccos, csin, mix, *waves, *extra),
        [
            pltpu.VMEM((plan.planes, share, cols), jnp.float32),
            pltpu.VMEM((channels + 2 * HALO, share, cols), jnp.float32),
            pltpu.VMEM((channels * kernels * (HALO + 1), 8, LANES), jnp.float32),
            pltpu.VMEM((chans, share, width), jnp.bfloat16),
        ],
        smem=(0, 1), name="detect",
    )
    out = jnp.zeros((local_chans, local_rows, cols), jnp.bfloat16)
    for k, block in enumerate(exchange(best)):
        out = lax.dynamic_update_slice_in_dim(out, block, (place ^ k) * share, axis=1)
    return out


def solution(mesh):
    in_specs = (P(("groups", "chan"), "space", None), P(None, "space"), P())
    out_specs = P(("groups", "chan"), "space", None)
    return jax.shard_map(local, mesh=mesh, in_specs=in_specs, out_specs=out_specs, check_vma=False)
```

```python
import functools
import math

import jax
import jax.numpy as jnp
import ml_dtypes
import numpy as np
from jax import lax
from jax.experimental import pallas as pl
from jax.experimental.pallas import tpu as pltpu
from jax.sharding import PartitionSpec as P

ORDER = 8
HALO = 2
LANES = 128
BF16 = ml_dtypes.bfloat16


def continuum_complement(channels):
    pos = np.arange(channels, dtype=np.float64)
    xval = -1.0 + (2.0 * pos + 1.0) / channels
    columns = [np.ones_like(xval), xval]
    for degree in range(1, ORDER):
        columns.append(
            ((2.0 * degree + 1.0) * xval * columns[degree] - degree * columns[degree - 1])
            / (degree + 1.0)
        )

    def orthogonal(vector, done):
        for _ in range(2):
            for prior in done:
                vector = vector - np.sum(prior * vector) * prior
        return vector

    sides = []
    for parity in (0, 1):
        done = []
        for column in columns[parity::2]:
            vector = orthogonal(column, done)
            done.append(vector / np.sqrt(np.sum(vector * vector)))
        wanted = channels // 2 - len(done)
        seeds = []
        for c in range(channels // 2):
            seed = np.zeros(channels)
            seed[c] = 1.0
            seed[channels - 1 - c] = 1.0 - 2.0 * parity
            seeds.append(seed)
        found = []
        for _ in range(wanted):
            rest = [orthogonal(seed, done) for seed in seeds]
            sizes = [float(np.sum(vector * vector)) for vector in rest]
            best = int(np.argmax(sizes))
            vector = rest[best] / math.sqrt(sizes[best])
            done.append(vector)
            found.append(vector)
        sides.append(found)
    return np.stack(sides[0] + sides[1], axis=1), len(sides[0])


def dft_table(left, right, length):
    phase = (left[:, None] * right[None, :] % length) * (2.0 * math.pi / length)
    return np.cos(phase).astype(BF16), np.sin(phase).astype(BF16)


def kernel_taps(widths, reach):
    offset = jnp.arange(-reach, reach + 1, dtype=jnp.int32).astype(jnp.float32)
    shape = jnp.exp(-offset[None, :] ** 2 / (2.0 * widths[:, None] ** 2))
    return (shape / jnp.sqrt(jnp.sum(shape * shape, axis=1, keepdims=True))).astype(jnp.bfloat16)


def iota(shape, axis):
    return lax.broadcasted_iota(jnp.int32, shape, axis)


class Plan:
    def __init__(self, chans, spaces, local_chans, local_rows, cols):
        self.chans, self.spaces = chans, spaces
        self.local_chans = local_chans
        self.channels = local_chans * chans
        self.rows = local_rows * spaces
        self.cols = cols
        self.share = local_rows // chans
        self.comp, self.evens = continuum_complement(self.channels)
        self.planes = self.comp.shape[1]
        self.freqs = cols // 2 // chans
        self.slots = LANES // self.freqs
        self.groups = chans // self.slots
        self.part = -(-(self.planes * self.freqs + self.planes) // LANES) * LANES
        self.width = 2 * self.part
        self.gram_rows = -(-self.planes // 8) * 8
        self.gram_cols = -(-self.planes // LANES) * LANES
        self.ride = (
            self.planes <= 8 <= self.freqs
            and self.planes < self.part // self.freqs
            and self.share >= 32
        )
        assert spaces == 2 and chans & (chans - 1) == 0 and self.groups * self.slots == chans


def slot_of(plan, shape):
    return lax.shift_right_logical(
        iota(shape, len(shape) - 1), int(math.log2(plan.freqs))
    )


def cut_kernel(plan, place_ref, cube_ref, *refs):
    outs, sems = refs[: plan.chans], refs[plan.chans]
    copies = []
    for k in range(plan.chans):
        row = pl.multiple_of((place_ref[0] ^ k) * plan.share, plan.share)
        copies.append(
            pltpu.make_async_copy(cube_ref.at[:, pl.ds(row, plan.share), :], outs[k], sems.at[k])
        )
    for copy in copies:
        copy.start()
    for copy in copies:
        copy.wait()


def spectra_kernel(plan, place_ref, *refs):
    cubes, refs = refs[: plan.chans], refs[plan.chans :]
    comp_ref, cos_ref, sin_ref = refs[:3]
    outs, (fit_ref, block_ref) = refs[3 : 3 + plan.chans], refs[3 + plan.chans :]
    share, cols, own = plan.share, plan.cols, plan.local_chans
    lane_tiles = cols // LANES

    def project(step, carry):
        row = pl.multiple_of((step // lane_tiles) * 16, 16)
        col = pl.multiple_of((step % lane_tiles) * LANES, LANES)
        sums, difs = [], []
        for k in range(plan.chans // 2):
            for c in range(own):
                one = cubes[k][c, pl.ds(row, 16), pl.ds(col, LANES)]
                two = cubes[k ^ (plan.chans - 1)][own - 1 - c, pl.ds(row, 16), pl.ds(col, LANES)]
                one, two = (v.astype(jnp.float32).reshape(2, 8, LANES) for v in (one, two))
                sums.append(one + two)
                difs.append(one - two)
        for j in range(plan.planes):
            total = None
            for at, value in enumerate(sums if j < plan.evens else difs):
                term = value * comp_ref[at * plan.planes + j][None]
                total = term if total is None else total + term
            fit_ref[j, pl.ds(row, 16), pl.ds(col, LANES)] = total.reshape(16, LANES).astype(
                jnp.bfloat16
            )
        return carry

    lax.fori_loop(0, (share // 16) * lane_tiles, project, 0)
    fits = fit_ref[...].reshape(plan.planes * share, cols)
    real = jnp.dot(fits, cos_ref[:, : cols // 2], preferred_element_type=jnp.float32)
    imag = -jnp.dot(fits, sin_ref[:, : cols // 2], preferred_element_type=jnp.float32)
    sign = (1 - 2 * (iota((cols, LANES), 0) & 1)).astype(jnp.bfloat16)
    last = jnp.dot(fits, sign, preferred_element_type=jnp.float32)
    slot = slot_of(plan, (share, LANES))
    lane = iota((share, LANES), 1)
    for part, spec in enumerate((real, imag)):
        for group in range(plan.groups):
            turned = []
            for j in range(plan.planes):
                block = spec[j * share : (j + 1) * share, group * LANES : (group + 1) * LANES]
                shift = plan.freqs * (j % plan.slots)
                turned.append(pltpu.roll(block, shift, 1) if shift else block)
            for e in range(plan.slots):
                dest = group * plan.slots + e
                for tile in range(plan.part // LANES):
                    value = jnp.zeros((share, LANES), jnp.float32)
                    for j in range(tile * plan.slots, min((tile + 1) * plan.slots, plan.planes)):
                        value = jnp.where(slot == (e + j) % plan.slots, turned[j], value)
                    if dest == 0 and part == 0:
                        for j in range(plan.planes):
                            at = plan.planes * plan.freqs + j
                            if at // LANES == tile:
                                value = jnp.where(
                                    lane == at % LANES, last[j * share : (j + 1) * share], value
                                )
                    start = part * plan.part + tile * LANES
                    block_ref[dest, :, start : start + LANES] = value.astype(jnp.bfloat16)
    for k in range(plan.chans):
        outs[k][...] = block_ref[place_ref[0] ^ k]


def lane_facts(plan, place, shape, axis):
    lane = iota(shape, axis)
    part = (lane >= plan.part).astype(jnp.int32)
    local = lane - part * plan.part
    slot = lax.shift_right_logical(local & (LANES - 1), int(math.log2(plan.freqs)))
    plane = lax.shift_right_logical(local, 7) * plan.slots + ((slot - place) & (plan.slots - 1))
    freq = local & (plan.freqs - 1)
    base = plan.planes * plan.freqs
    own = (local >= base) & (local < base + plan.planes) & (place == 0)
    plane = jnp.where(own, local - base, plane)
    freq = jnp.where(own, plan.freqs, freq)
    single = own | ((place == 0) & (freq == 0))
    return part, freq, plane, jnp.where(single, (1 - part) * plan.cols, plan.cols // 2)


def rider_of(gram):
    first = gram.astype(jnp.bfloat16).astype(jnp.float32)
    second = (gram - first).astype(jnp.bfloat16).astype(jnp.float32)
    third = gram - first - second
    return jnp.concatenate([first, second, third, jnp.zeros_like(first)], axis=0)


def free_tile(plan):
    return plan.part + plan.planes // plan.slots * LANES


def smooth_kernel(plan, place_ref, side_ref, fwd_ref, inv_ref, beam_ref, *refs):
    count = plan.chans
    mine, theirs, refs = refs[:count], refs[count : 2 * count], refs[2 * count :]
    out_ref, gram_ref, fold_ref = refs
    place, side = place_ref[0], side_ref[0]
    quarter, width, share, half = plan.rows // 4, plan.width, plan.share, plan.chans // 2
    odd = side.astype(jnp.float32)
    even = 1.0 - odd
    sigma = even - odd

    def turn(value):
        return jnp.concatenate([value[:, plan.part :], -value[:, : plan.part]], axis=1)

    for k in range(count):
        fold_ref[place ^ k] = theirs[k][...].astype(jnp.float32) + sigma * mine[k][...].astype(
            jnp.float32
        )
    low = fold_ref[0:half].reshape(quarter, width)
    high = fold_ref[half:].reshape(quarter, width)
    high = even * high + odd * turn(high)
    waves = []
    for at, value in enumerate((low + high, low - high)):
        data = jnp.concatenate([value, turn(value)], axis=0).astype(jnp.bfloat16)
        value = jnp.dot(fwd_ref[2 * side + at], data, preferred_element_type=jnp.float32)
        value = value * beam_ref[at]
        data = jnp.concatenate([value, turn(value)], axis=0).astype(jnp.bfloat16)
        waves.append(
            jnp.dot(inv_ref[2 * side + at], data, preferred_element_type=jnp.float32)
        )
    rest = waves[0] - waves[1]
    low = (waves[0] + waves[1]).astype(jnp.bfloat16)
    high = (even * rest - odd * turn(rest)).astype(jnp.bfloat16)
    out_ref[0:half] = low.reshape(half, share, width)
    out_ref[half:] = high.reshape(half, share, width)
    both = jnp.concatenate([low, high], axis=0)
    part, freq, plane, weight = lane_facts(plan, place, (1, width), 1)
    _, cfreq, cplane, _ = lane_facts(plan, place, (width, 1), 0)
    weighted = both * (2 * weight).astype(jnp.bfloat16)
    high_p = lax.Precision.HIGHEST
    if plan.ride:
        free = (place + plan.planes) & (plan.slots - 1)
    else:
        free = 0
    gram = None
    for at in range(2):
        lanes = slice(at * plan.part, (at + 1) * plan.part)
        cross = lax.dot_general(
            both[:, lanes], weighted[:, lanes], (((0,), (0,)), ((), ())),
            preferred_element_type=jnp.float32,
        )
        cross = jnp.where(freq[:, lanes] == cfreq[lanes], cross, 0.0)
        rows_of = (iota((plan.gram_rows, plan.part), 0) == plane[:, lanes]).astype(jnp.float32)
        target = iota((plan.part, plan.gram_cols), 1) - free * plan.freqs
        cols_of = ((target == cplane[lanes]) & (target < plan.planes)).astype(jnp.float32)
        cross = jnp.dot(rows_of, cross, precision=high_p, preferred_element_type=jnp.float32)
        cross = jnp.dot(cross, cols_of, precision=high_p, preferred_element_type=jnp.float32)
        gram = cross if gram is None else gram + cross
    gram_ref[...] = gram
    if plan.ride:
        tile = slice(free_tile(plan), free_tile(plan) + LANES)
        inside = slot_of(plan, (32, LANES)) == free
        now = out_ref[0, 0:32, tile].astype(jnp.float32)
        out_ref[0, 0:32, tile] = jnp.where(inside, rider_of(gram), now).astype(jnp.bfloat16)


def merge_kernel(plan, place_ref, side_ref, mine_ref, theirs_ref, gram_ref, *outs):
    place = place_ref[0]
    sigma = 1.0 - 2.0 * side_ref[0].astype(jnp.float32)
    for k in range(plan.chans):
        at = place ^ k
        value = theirs_ref[at].astype(jnp.float32) + sigma * mine_ref[at].astype(jnp.float32)
        outs[k][...] = value.astype(jnp.bfloat16)
    if plan.ride:
        tile = slice(free_tile(plan), free_tile(plan) + LANES)
        inside = slot_of(plan, (32, LANES)) == ((place + plan.planes) & (plan.slots - 1))
        other = theirs_ref[0, 0:32, tile].astype(jnp.float32)
        rider = rider_of(gram_ref[...] + other[0:8] + other[8:16] + other[16:24])
        for k in range(plan.chans):
            now = outs[k][0:32, tile].astype(jnp.float32)
            outs[k][0:32, tile] = jnp.where(inside, rider, now).astype(jnp.bfloat16)


def smooth_planes(plan, place, blocks, wave_ref, icos_ref, isin_ref):
    share, cols = plan.share, plan.cols
    for k in range(plan.chans):
        wave_ref[place ^ k] = blocks[k][...]
    slot = slot_of(plan, (share, LANES))
    lane = iota((share, LANES), 1)
    gram = None
    if plan.ride:
        gram = jnp.zeros((24, LANES), jnp.float32)
        free = slot_of(plan, (24, LANES))
        tile = slice(free_tile(plan), free_tile(plan) + LANES)
        for e in range(plan.slots):
            at = (e + plan.planes) % plan.slots
            total = jnp.zeros((24, LANES), jnp.float32)
            for group in range(plan.groups):
                block = wave_ref[group * plan.slots + e, 0:32, tile]
                total += block.astype(jnp.float32)[0:24]
            total = jnp.where(free == at, total, 0.0)
            shift = (LANES - at * plan.freqs) % LANES
            gram += pltpu.roll(total, shift, 1) if shift else total
        gram = gram[0:8] + gram[8:16] + gram[16:24]
        gram = jnp.concatenate([gram, jnp.zeros((LANES - 8, LANES), jnp.float32)], axis=0)
    pieces = []
    for j in range(plan.planes):
        tile, shift = j // plan.slots, (LANES - plan.freqs * (j % plan.slots)) % LANES
        line = []
        for part in range(2):
            start = part * plan.part + tile * LANES
            for group in range(plan.groups):
                value = jnp.zeros((share, LANES), jnp.float32)
                for e in range(plan.slots):
                    block = wave_ref[group * plan.slots + e, :, start : start + LANES]
                    value = jnp.where(
                        slot == (e + j) % plan.slots, block.astype(jnp.float32), value
                    )
                line.append((pltpu.roll(value, shift, 1) if shift else value).astype(jnp.bfloat16))
        at = plan.planes * plan.freqs + j
        start = at // LANES * LANES
        block = wave_ref[0, :, start : start + LANES].astype(jnp.float32)
        line.append(jnp.where(lane == at % LANES, block, 0.0).astype(jnp.bfloat16))
        pieces.append(jnp.concatenate(line, axis=1))
    data = jnp.concatenate(pieces, axis=0)
    count = cols // 2
    sign = (1 - 2 * (iota((LANES, cols), 1) & 1)).astype(jnp.bfloat16)
    smooth = (
        jnp.dot(data[:, :count], icos_ref[:count, :], preferred_element_type=jnp.float32)
        - jnp.dot(data[:, count:cols], isin_ref[:count, :], preferred_element_type=jnp.float32)
        + jnp.dot(data[:, cols:], sign, preferred_element_type=jnp.float32)
    )
    return smooth.reshape(plan.planes, share, cols), gram


def detect_kernel(plan, place_ref, taps_ref, icos_ref, isin_ref, mix_ref, *refs):
    blocks, refs = refs[: plan.chans], refs[plan.chans :]
    if not plan.ride:
        gram_ref, refs = refs[0], refs[1:]
    outs, (plane_ref, chan_ref, scale_ref, wave_ref) = refs[: plan.chans], refs[plan.chans :]
    place = place_ref[0]
    share, cols = plan.share, plan.cols
    kernels = taps_ref.shape[0]
    channels, half = plan.channels, plan.channels // 2
    smooth, gram = smooth_planes(plan, place, blocks, wave_ref, icos_ref, isin_ref)
    plane_ref[...] = smooth
    if not plan.ride:
        gram = gram_ref[...]
    mix = mix_ref[...]
    power = jnp.dot(mix, gram, precision=lax.Precision.HIGHEST, preferred_element_type=jnp.float32)
    power = jnp.sum(power * mix, axis=1, keepdims=True) / (plan.rows * plan.cols)
    scale = 1.0 / jnp.sqrt(jnp.maximum(power, 0.0) + 1e-06)
    scale = jnp.broadcast_to(scale, (kernels * channels, LANES))
    for k in range(kernels):
        for c in range(channels):
            row = jnp.broadcast_to(scale[k * channels + c : k * channels + c + 1], (8, LANES))
            for j in range(HALO + 1):
                scale_ref[(c * kernels + k) * (HALO + 1) + j] = row * taps_ref[k, HALO + j]

    comp = plan.comp
    lane_tiles = cols // LANES

    own = plan.local_chans
    edge = jnp.zeros((HALO, share, cols), jnp.float32)
    chan_ref[0:HALO] = edge
    chan_ref[HALO + channels :] = edge

    def expand(step, carry):
        row = pl.multiple_of((step // lane_tiles) * 16, 16)
        col = pl.multiple_of((step % lane_tiles) * LANES, LANES)
        planes = [
            plane_ref[j, pl.ds(row, 16), pl.ds(col, LANES)].reshape(2, 8, LANES)
            for j in range(plan.planes)
        ]
        for c in range(half):
            even = odd = None
            for j in range(plan.planes):
                term = planes[j] * float(comp[c, j])
                if j < plan.evens:
                    even = term if even is None else even + term
                else:
                    odd = term if odd is None else odd + term
            for at, value in ((c, even + odd), (channels - 1 - c, even - odd)):
                chan_ref[HALO + at, pl.ds(row, 16), pl.ds(col, LANES)] = value.reshape(16, LANES)
        return carry

    def respond(step, carry):
        row = pl.multiple_of((step // lane_tiles) * 16, 16)
        col = pl.multiple_of((step % lane_tiles) * LANES, LANES)
        for block in range(plan.chans):
            first = (place ^ block) * own
            near = [
                chan_ref[first + at, pl.ds(row, 16), pl.ds(col, LANES)].reshape(2, 8, LANES)
                for at in range(own + 2 * HALO)
            ]
            for c in range(own):
                mid = c + HALO
                sums = [near[mid]]
                for j in range(1, HALO + 1):
                    sums.append(near[mid - j] + near[mid + j])
                best = None
                for k in range(kernels):
                    value = None
                    for j in range(HALO + 1):
                        at = ((first + c) * kernels + k) * (HALO + 1) + j
                        term = sums[j] * scale_ref[at][None]
                        value = term if value is None else value + term
                    best = value if best is None else jnp.maximum(best, value)
                outs[block][c, pl.ds(row, 16), pl.ds(col, LANES)] = best.reshape(
                    16, LANES
                ).astype(jnp.bfloat16)
        return carry

    lax.fori_loop(0, (share // 16) * lane_tiles, expand, 0)
    lax.fori_loop(0, (share // 16) * lane_tiles, respond, 0)


def call(kernel, out_shape, args, scratch=(), smem=(), hbm=(), name=None, room=20):
    vmem = pl.BlockSpec(memory_space=pltpu.VMEM)
    return pl.pallas_call(
        kernel,
        out_shape=out_shape,
        in_specs=[
            pl.BlockSpec(memory_space=pltpu.SMEM if at in smem else pl.ANY if at in hbm else pltpu.VMEM)
            for at in range(len(args))
        ],
        out_specs=jax.tree.map(lambda _: vmem, out_shape),
        scratch_shapes=list(scratch),
        compiler_params=pltpu.CompilerParams(vmem_limit_bytes=room << 20),
        name=name,
    )(*args)


def own_beam(plan, beam, place, side):
    rows, cols, freqs = plan.rows, plan.cols, plan.freqs
    at = np.arange(freqs + 1)
    freq = place * freqs + at
    column = jnp.where(side == 0, freq, cols // 2 - freq)
    column = jnp.where(at == freqs, 0, column)
    pick = (jnp.arange(cols // 2)[:, None] == column[None, :]).astype(jnp.float32)
    high_p = lax.Precision.HIGHEST
    found = jnp.dot(beam, pick, precision=high_p)
    found = found.reshape(rows // 4, 4, -1).transpose(1, 0, 2)
    flip = found[::-1, ::-1]
    flip = jnp.concatenate([jnp.roll(flip[3:], 1, axis=1), flip[:3]], axis=0)
    plain = (side == 0) | (at == freqs)
    found = jnp.where(plain, found, flip)
    found = found.reshape(2, 2, rows // 4, freqs + 1)
    mine = jnp.where(side == 0, found[:, 0], found[:, 1])
    yours = jnp.where(side == 0, found[:, 1], found[:, 0])
    other = lax.ppermute(yours, "space", [(0, 1), (1, 0)])
    last = jnp.where(side == 0, other, mine)[:, :, freqs:]
    total = jnp.concatenate([(mine + other)[:, :, :freqs], last], axis=2)
    lane = np.arange(plan.width)
    base = plan.planes * freqs
    local = lane % plan.part
    own = (place == 0) & (local >= base) & (local < base + plan.planes)
    source = jnp.where(own, freqs, lane % freqs)
    pick = (np.arange(freqs + 1)[:, None] == source[None, :]) * np.float32(1.0 / (rows * cols))
    return jnp.dot(total, pick, precision=high_p)


def transpose_kernel(fwd_ref, inv_ref):
    count, size, _ = fwd_ref.shape
    for rest in range(count):
        cos = fwd_ref[rest, :, :size].astype(jnp.float32)
        sin = fwd_ref[rest, :, size:].astype(jnp.float32)
        inv_ref[rest, :, :size] = cos.T.astype(jnp.bfloat16)
        inv_ref[rest, :, size:] = (-sin.T).astype(jnp.bfloat16)


def exchange(blocks):
    count = len(blocks)
    moved = list(blocks)
    for k in (*range(count // 2, count), *range(count // 4, count // 2), *range(1, count // 4)):
        moved[k] = lax.ppermute(blocks[k], "chan", [(a, a ^ k) for a in range(count)])
    return moved


def swap(block):
    return lax.ppermute(block, "space", [(0, 1), (1, 0)])


def local(cube, beam_response, line_widths):
    local_chans, local_rows, cols = cube.shape
    chans, spaces = lax.axis_size("chan"), lax.axis_size("space")
    plan = Plan(chans, spaces, local_chans, local_rows, cols)
    rows, share, width, channels = plan.rows, plan.share, plan.width, plan.channels
    side, place = lax.axis_index("space"), lax.axis_index("chan")
    sides, places = (v.reshape(1).astype(jnp.int32) for v in (side, place))
    steps = np.arange(rows // 4, dtype=np.int64)
    ccos, csin = dft_table(np.arange(cols), np.arange(cols), cols)
    fwd = [np.concatenate(dft_table(4 * steps + r, steps, rows), axis=1) for r in (0, 2, 1, 3)]
    ccos, csin, fwd = jnp.asarray(ccos), jnp.asarray(csin), jnp.asarray(np.stack(fwd))

    cube_shape = jax.ShapeDtypeStruct((local_chans, share, cols), jnp.bfloat16)
    block_shape = jax.ShapeDtypeStruct((share, width), jnp.bfloat16)
    wave_shape = jax.ShapeDtypeStruct((chans, share, width), jnp.bfloat16)
    gram_shape = jax.ShapeDtypeStruct((plan.gram_rows, plan.gram_cols), jnp.float32)
    blocks = call(
        functools.partial(cut_kernel, plan), [cube_shape] * chans, (places, cube),
        [pltpu.SemaphoreType.DMA((chans,))], smem=(0,), hbm=(1,), name="cut",
    )
    moved = exchange(blocks)
    first = chans // 2
    moved[first], beam_response, table, widths = lax.optimization_barrier(
        (moved[first], beam_response, fwd, line_widths)
    )
    pairs = plan.comp.reshape(chans, local_chans * plan.planes).astype(np.float32)
    comp = jnp.asarray(pairs)[place ^ np.arange(chans // 2)]
    comp = jnp.broadcast_to(comp.reshape(-1, 1, 1), (comp.size, 8, LANES))
    beam = own_beam(plan, beam_response, place, side)
    inv = call(transpose_kernel, jax.ShapeDtypeStruct(fwd.shape, fwd.dtype), (table,), name="tables")
    taps = kernel_taps(widths, HALO).astype(jnp.float32)
    padded = np.pad(plan.comp, ((HALO, HALO), (0, 0))).astype(np.float32)
    mix = sum(taps[:, j, None, None] * padded[None, j : j + channels] for j in range(2 * HALO + 1))
    mix = mix.reshape(-1, plan.planes)
    mix = jnp.pad(mix, ((0, 0), (0, -plan.planes % LANES)))
    moved[0], beam, inv, mix, taps, comp = lax.optimization_barrier(
        (moved[0], beam, inv, mix, taps, comp)
    )
    spectra = call(
        functools.partial(spectra_kernel, plan), [block_shape] * chans,
        (places, *moved, comp, ccos, csin),
        [
            pltpu.VMEM((plan.planes, share, cols), jnp.bfloat16),
            pltpu.VMEM((chans, share, width), jnp.bfloat16),
        ],
        smem=(0,), name="spectra",
    )
    spectra = exchange(spectra)
    theirs = [swap(block) for block in spectra]
    wave, gram = call(
        functools.partial(smooth_kernel, plan), (wave_shape, gram_shape),
        (places, sides, fwd, inv, beam, *spectra, *theirs),
        [pltpu.VMEM((chans, share, width), jnp.float32)], smem=(0, 1), name="smooth",
    )
    waves = call(
        functools.partial(merge_kernel, plan), [block_shape] * chans,
        (places, sides, wave, swap(wave), gram), smem=(0, 1), name="merge",
    )
    waves = exchange(waves)
    extra = ()
    if not plan.ride:
        gram = lax.psum(gram, ("chan", "space"))
        extra = (jnp.pad(gram, ((0, gram.shape[1] - gram.shape[0]), (0, 0))),)
    kernels = taps.shape[0]
    best = call(
        functools.partial(detect_kernel, plan), [cube_shape] * chans,
        (places, taps, ccos, csin, mix, *waves, *extra),
        [
            pltpu.VMEM((plan.planes, share, cols), jnp.float32),
            pltpu.VMEM((channels + 2 * HALO, share, cols), jnp.float32),
            pltpu.VMEM((channels * kernels * (HALO + 1), 8, LANES), jnp.float32),
            pltpu.VMEM((chans, share, width), jnp.bfloat16),
        ],
        smem=(0, 1), name="detect",
    )
    out = jnp.zeros((local_chans, local_rows, cols), jnp.bfloat16)
    for k, block in enumerate(exchange(best)):
        out = lax.dynamic_update_slice_in_dim(out, block, (place ^ k) * share, axis=1)
    return out


def solution(mesh):
    in_specs = (P(("groups", "chan"), "space", None), P(None, "space"), P())
    out_specs = P(("groups", "chan"), "space", None)
    return jax.shard_map(local, mesh=mesh, in_specs=in_specs, out_specs=out_specs, check_vma=False)
```
